32 devices in a mesh: dp: 4 (over z), seq: 8 (over y, x, core).
Axes of the slice: x: 2, y: 2, z: 4, core: 2. Of those that a mesh axis runs over, the one named last changes fastest.
Arguments:
- queries: bfloat16 [4096, 1024], P(('dp', 'seq')), may hold values from -6 to 6
- keys: bfloat16 [4096, 128], P(('dp', 'seq')), may hold values from -6 to 6
- values: bfloat16 [4096, 128], P(('dp', 'seq')), may hold values from -6 to 6
- d_out: bfloat16 [4096, 1024], P(('dp', 'seq')), may hold values from -6 to 6
- doc_lengths: int32 [11], replicated, may hold values from 1 to 768, as said below
Outputs:
- d_queries: bfloat16 [4096, 1024], P(('dp', 'seq'))
- key_gradient: bfloat16 [4096, 128], P(('dp', 'seq'))
- value_gradient: bfloat16 [4096, 128], P(('dp', 'seq'))
The draws below stay inside these ranges and needn't reach their ends.
Inputs may be any that keep to these rules, and one draw needn't show every extreme that they name: `doc_lengths`: lengths of the 11 documents in order; they sum to 4096, and the longest has exactly 768 tokens.
All inputs are finite; a program needn't handle non-finite values.
Results may differ from the reference program's by a relative error of at most 0.008.
Values may be sent and summed in bfloat16 or wider, within the bound.
No kernel may reach another device: no remote copies, remote signals or barrier semaphores. Data moves between devices by JAX's collectives and lax.ppermute only.
A program may use at most 64 MiB of HBM per device.

```python
import math
import jax
import jax.numpy as jnp
from jax import lax

HEAD_SIZE = 128
GROUP = 8
DOC_MOST = 768
HQ = 8
KEY_VALUE_HEADS = 1
PACKED_TOKENS = 4096
NDOC = 11


def lengths_from(key):
    others_count = NDOC - 1
    leftover = PACKED_TOKENS - DOC_MOST - others_count
    middle = leftover // others_count
    surplus = leftover % others_count
    spread_max = min(middle, DOC_MOST - 2 - middle)
    shifts = jax.random.randint(jax.random.fold_in(key, 11), (others_count // 2,), -spread_max, spread_max + 1, dtype=jnp.int32)
    pieces = jnp.concatenate([shifts, -shifts])
    bumped = (jnp.arange(others_count, dtype=jnp.int32) < surplus).astype(jnp.int32)
    others = 1 + middle + pieces + bumped
    all_lengths = jnp.concatenate([jnp.full((1,), DOC_MOST, jnp.int32), others])
    shuffle = jax.random.permutation(jax.random.fold_in(key, 12), NDOC)
    return all_lengths[shuffle]


def draw_doc_lengths(key, part):
    return lengths_from(key)


def draw_keys(key, part):
    sampled_draw = jnp.clip(jax.random.normal(jax.random.fold_in(key, 22), (PACKED_TOKENS, KEY_VALUE_HEADS, HEAD_SIZE), jnp.float32), -6.0, 6.0)
    return sampled_draw.reshape(PACKED_TOKENS, KEY_VALUE_HEADS * HEAD_SIZE).astype(jnp.bfloat16)


def draw_queries(key, part):
    sampled_draw = jnp.clip(jax.random.normal(jax.random.fold_in(key, 21), (PACKED_TOKENS, HQ, HEAD_SIZE), jnp.float32), -6.0, 6.0)
    return sampled_draw.reshape(PACKED_TOKENS, HQ * HEAD_SIZE).astype(jnp.bfloat16)


def block_scale(rng, shape, split, least, high):
    gain, own = 1.0, jax.random.fold_in(rng, 6)
    for dim, shards_of in split:
        steps = jnp.exp(jax.random.uniform(jax.random.fold_in(own, dim), (shards_of,), jnp.float32, least / len(split), high / len(split)))
        gain = gain * jnp.repeat(steps, shape[dim] // shards_of).reshape([-1 if axis == dim else 1 for axis in range(len(shape))])
    return gain


def scatter_about(rng, extent, width, most, cuts=(), held_as=jnp.bfloat16):
    loudness = block_scale(rng, extent, cuts, -0.22, 0.18) if cuts else 1.0
    result = jax.random.normal(rng, extent, jnp.float32) * width * loudness
    return jnp.minimum(jnp.maximum(result, -most), most).astype(held_as)


def setup_inputs(seed: int = 0) -> dict:
    splits = jax.random.split(jax.random.key(seed), 6)
    return {
        "queries": draw_queries(jax.random.fold_in(splits[5], 71), 0),
        "keys": draw_keys(jax.random.fold_in(splits[5], 71), 0),
        "values": scatter_about(splits[2], (PACKED_TOKENS, KEY_VALUE_HEADS * HEAD_SIZE), 1.0, 6.0, ((0, 32),)),
        "d_out": scatter_about(splits[3], (PACKED_TOKENS, HQ * HEAD_SIZE), 1.0, 6.0, ((0, 32),)),
        "doc_lengths": draw_doc_lengths(jax.random.fold_in(splits[5], 71), 0),
    }


def doc_index(positions, doc_ends):
    return lax.optimization_barrier(jnp.sum((positions[:, None] >= doc_ends[None, :]).astype(jnp.int32), axis=1))

def block_grads(q_rows, key_rows, value_rows, grad_rows, allowed, score_scale):
    scores = jnp.dot(q_rows, key_rows.T, preferred_element_type=jnp.float32) * score_scale
    scores = jnp.where(allowed, scores, -1e+30)
    row_max = lax.optimization_barrier(jnp.max(scores, axis=1, keepdims=True))
    exp_scores = jnp.exp(scores - row_max)
    attn_probs = exp_scores / lax.optimization_barrier(jnp.sum(exp_scores, axis=1, keepdims=True))
    probs_low = attn_probs.astype(jnp.bfloat16)
    grad_probs = jnp.dot(grad_rows, value_rows.T, preferred_element_type=jnp.float32)
    row_delta = lax.optimization_barrier(jnp.sum(attn_probs * grad_probs, axis=1, keepdims=True))
    grad_scores = (attn_probs * (grad_probs - row_delta) * score_scale).astype(jnp.bfloat16)
    grad_q = jnp.dot(grad_scores, key_rows, preferred_element_type=jnp.float32)
    grad_k = jnp.dot(grad_scores.T, q_rows, preferred_element_type=jnp.float32)
    grad_v = jnp.dot(probs_low.T, grad_rows, preferred_element_type=jnp.float32)
    return (grad_q, grad_k, grad_v)

def reference(queries, keys, values, d_out, doc_lengths):
    grand_total = queries.shape[0]
    doc_ends = jnp.cumsum(doc_lengths).astype(jnp.int32)
    query_span = min(512, grand_total)
    key_window = min(query_span + DOC_MOST, grand_total)
    steps_count = grand_total // query_span
    positions = jnp.arange(grand_total, dtype=jnp.int32)
    all_docs = doc_index(positions, doc_ends)
    q_heads = queries.reshape(grand_total, HQ, HEAD_SIZE)
    g_heads = d_out.reshape(grand_total, HQ, HEAD_SIZE)
    key_head_list = keys.reshape(grand_total, KEY_VALUE_HEADS, HEAD_SIZE)
    value_head_list = values.reshape(grand_total, KEY_VALUE_HEADS, HEAD_SIZE)
    score_scale = 1.0 / math.sqrt(HEAD_SIZE)

    def one_head(sums, head_index):
        key_sum_total, value_sum_total = sums
        q_head = lax.dynamic_index_in_dim(q_heads, head_index, 1, keepdims=False)
        g_head = lax.dynamic_index_in_dim(g_heads, head_index, 1, keepdims=False)
        kv_index = (head_index // GROUP).astype(jnp.int32)
        k_head = lax.dynamic_index_in_dim(key_head_list, kv_index, 1, keepdims=False)
        v_head = lax.dynamic_index_in_dim(value_head_list, kv_index, 1, keepdims=False)

        def step(totals, step_index):
            acc_k, acc_v = totals
            row_start = (step_index * query_span).astype(jnp.int32)
            key_start = jnp.clip(row_start - DOC_MOST, 0, grand_total - key_window).astype(jnp.int32)
            q_rows = lax.dynamic_slice_in_dim(q_head, row_start, query_span, 0)
            g_rows = lax.dynamic_slice_in_dim(g_head, row_start, query_span, 0)
            key_rows = lax.dynamic_slice_in_dim(k_head, key_start, key_window, 0)
            value_rows = lax.dynamic_slice_in_dim(v_head, key_start, key_window, 0)
            q_pos = lax.dynamic_slice_in_dim(positions, row_start, query_span, 0)
            k_pos = lax.dynamic_slice_in_dim(positions, key_start, key_window, 0)
            q_docs = lax.dynamic_slice_in_dim(all_docs, row_start, query_span, 0)
            k_docs = lax.dynamic_slice_in_dim(all_docs, key_start, key_window, 0)
            allowed = (q_docs[:, None] == k_docs[None, :]) & (k_pos[None, :] <= q_pos[:, None])
            grad_q, grad_k, grad_v = block_grads(q_rows, key_rows, value_rows, g_rows, allowed, score_scale)
            acc_k = lax.dynamic_update_slice_in_dim(acc_k, lax.dynamic_slice_in_dim(acc_k, key_start, key_window, 0) + grad_k, key_start, 0)
            acc_v = lax.dynamic_update_slice_in_dim(acc_v, lax.dynamic_slice_in_dim(acc_v, key_start, key_window, 0) + grad_v, key_start, 0)
            return ((acc_k, acc_v), grad_q.astype(jnp.bfloat16))
        empty_acc = jnp.zeros((grand_total, HEAD_SIZE), jnp.float32)
        (acc_k, acc_v), q_blocks = lax.scan(step, (empty_acc, empty_acc), jnp.arange(steps_count, dtype=jnp.int32))
        key_sum_total = key_sum_total.at[kv_index].add(acc_k)
        value_sum_total = value_sum_total.at[kv_index].add(acc_v)
        return ((key_sum_total, value_sum_total), q_blocks.reshape(grand_total, HEAD_SIZE))
    initial_sum = jnp.zeros((KEY_VALUE_HEADS, grand_total, HEAD_SIZE), jnp.float32)
    (key_sum_total, value_sum_total), grad_q = lax.scan(one_head, (initial_sum, initial_sum), jnp.arange(HQ, dtype=jnp.int32))
    d_queries = jnp.transpose(grad_q, (1, 0, 2)).reshape(grand_total, HQ * HEAD_SIZE)
    key_gradient = jnp.transpose(key_sum_total, (1, 0, 2)).reshape(grand_total, KEY_VALUE_HEADS * HEAD_SIZE).astype(jnp.bfloat16)
    value_gradient = jnp.transpose(value_sum_total, (1, 0, 2)).reshape(grand_total, KEY_VALUE_HEADS * HEAD_SIZE).astype(jnp.bfloat16)
    return (d_queries, key_gradient, value_gradient)
```

```python
import functools
import math

import jax
import jax.numpy as jnp
from jax import lax
from jax.experimental import pallas as pl
from jax.experimental.pallas import tpu as pltpu
from jax.sharding import PartitionSpec as P

HEAD_SIZE = 128
GROUP = 8
DOC_MOST = 768
AXES = ("dp", "seq")
PAIRS_BACK = 3
SLOTS = 7
NEG = -1e30
F32 = jnp.float32
BF16 = jnp.bfloat16


def permute(value, devices, source_of):
    moves = [(source_of(d), d) for d in range(devices) if 0 <= source_of(d) < devices]
    return lax.ppermute(value, AXES, moves)


def permute_back(value, devices, source_of):
    moves = [(d, source_of(d)) for d in range(devices) if 0 <= source_of(d) < devices]
    return lax.ppermute(value, AXES, moves)


def mate_of(d):
    return d ^ 1


def near_of(d):
    return d - 2 if d % 2 == 0 else d - 4


def far_of(d):
    return d - 2 * PAIRS_BACK


def dot_nt(a, b):
    return lax.dot_general(a, b, (((1,), (1,)), ((), ())), preferred_element_type=F32)


def dot_nn(a, b):
    return lax.dot_general(a, b, (((1,), (0,)), ((), ())), preferred_element_type=F32)


def attention_kernel(
    rows,
    lens_ref,
    q_ref,
    g_ref,
    full_ref,
    near_ref,
    cross_ref,
    far_ref,
    dq_ref,
    own_ref,
    mate_ref,
    dnear_ref,
    dcross_ref,
    dfar_ref,
    qs,
    gs,
    kwin,
    vwin,
    kt,
    bias,
    sc,
    gp,
    pt,
    dst,
):
    t = rows
    scale = 1.0 / math.sqrt(HEAD_SIZE)
    scale2 = scale * math.log2(math.e)
    me = lax.axis_index("dp") * lax.axis_size("seq") + lax.axis_index("seq")
    odd = lax.rem(me, 2) == 1
    first = me * t
    for h in range(GROUP):
        qs[h * t : (h + 1) * t, :] = q_ref[:, h * HEAD_SIZE : (h + 1) * HEAD_SIZE]
        gs[h * t : (h + 1) * t, :] = g_ref[:, h * HEAD_SIZE : (h + 1) * HEAD_SIZE]
    pieces = (
        (full_ref, 0, 0, 0),
        (None, 0, 5, 1),
        (near_ref, 0, 2, 4),
        (near_ref, 2, 1, 5),
        (cross_ref, 0, 3, 3),
        (cross_ref, 2, 4, 2),
        (far_ref, 0, 6, 6),
    )
    q_pos = first + lax.broadcasted_iota(jnp.int32, (1, t), 1)

    def next_doc(j, carry):
        end, low = carry
        end = end + lens_ref[j]
        return end, jnp.where(end <= q_pos, end, low)

    _, low = lax.fori_loop(
        0, lens_ref.shape[0], next_doc, (jnp.int32(0), jnp.zeros((1, t), jnp.int32))
    )
    for slot, (ref, at, even_back, odd_back) in enumerate(pieces):
        if ref is None:
            key = jnp.where(odd, full_ref[2], far_ref[2])
            value = jnp.where(odd, full_ref[3], far_ref[3])
        else:
            key, value = ref[at], ref[at + 1]
        span = slice(slot * t, (slot + 1) * t)
        kwin[span, :] = key
        vwin[span, :] = value
        kt[:, span] = key.T
        back = jnp.where(odd, odd_back, even_back)
        k_pos = first - back * t + lax.broadcasted_iota(jnp.int32, (t, t), 0)
        allowed = k_pos >= low
        if slot == 0:
            allowed = allowed & (k_pos <= q_pos)
        bias[span, :] = jnp.where(allowed, 0.0, NEG)

    for pair in range(GROUP // 2):
        cols = slice(pair * 2 * t, (pair + 1) * 2 * t)
        sc[...] = dot_nt(kwin[...], qs[cols, :])
        gp[...] = dot_nt(vwin[...], gs[cols, :])
        top = None
        for slot in range(SLOTS):
            span = slice(slot * t, (slot + 1) * t)
            b = bias[span, :]
            s = sc[span, :] * scale2 + jnp.concatenate([b, b], axis=1)
            sc[span, :] = s
            high = jnp.max(s, axis=0, keepdims=True)
            top = high if top is None else jnp.maximum(top, high)
        total = jnp.zeros((1, 2 * t), F32)
        weighted = jnp.zeros((1, 2 * t), F32)
        for slot in range(SLOTS):
            span = slice(slot * t, (slot + 1) * t)
            e = jnp.exp2(sc[span, :] - top)
            sc[span, :] = e
            total += jnp.sum(e, axis=0, keepdims=True)
            weighted += jnp.sum(e * gp[span, :], axis=0, keepdims=True)
        inverse = 1.0 / total
        delta = weighted * inverse
        for slot in range(SLOTS):
            span = slice(slot * t, (slot + 1) * t)
            p = sc[span, :] * inverse
            ds = p * (gp[span, :] - delta) * scale
            pt[span, cols] = p.astype(BF16)
            dst[span, cols] = ds.astype(BF16)

    dk = dot_nn(dst[...], qs[...])
    dv = dot_nn(pt[...], gs[...])

    def part(grad, slot):
        return grad[slot * t : (slot + 1) * t, :]

    none = jnp.zeros((t, HEAD_SIZE), F32)
    for kind, grad in enumerate((dk, dv)):
        own_ref[kind] = part(grad, 0)
        mate_ref[kind] = jnp.where(odd, part(grad, 1), none)
        dnear_ref[kind] = part(grad, 2)
        dnear_ref[kind + 2] = part(grad, 3)
        dcross_ref[kind] = part(grad, 4).astype(BF16)
        dcross_ref[kind + 2] = part(grad, 5).astype(BF16)
        dfar_ref[kind] = part(grad, 6).astype(BF16)
        dfar_ref[kind + 2] = jnp.where(odd, none, part(grad, 1)).astype(BF16)
    dqt = dot_nn(kt[...], dst[...])
    for h in range(GROUP):
        dq_ref[:, h * HEAD_SIZE : (h + 1) * HEAD_SIZE] = dqt[:, h * t : (h + 1) * t].T.astype(BF16)


def local(queries, keys, values, d_out, doc_lengths):
    rows, q_width = queries.shape
    kv_width = keys.shape[1]
    kv_heads = kv_width // HEAD_SIZE
    devices = lax.axis_size("dp") * lax.axis_size("seq")
    mine = jnp.stack([keys, values])
    mate = permute(mine, devices, mate_of)
    full = jnp.concatenate([mine, mate], axis=0)
    near = permute(full, devices, near_of)
    far = permute(full, devices, far_of)
    cross = permute(near, devices, mate_of)

    wide = GROUP * HEAD_SIZE
    window = SLOTS * rows

    def cols(count):
        return pl.BlockSpec((count, rows, HEAD_SIZE), lambda g: (0, 0, g))

    heads = pl.BlockSpec((rows, wide), lambda g: (0, g))
    shape = jax.ShapeDtypeStruct
    d_queries, own, own_mate, d_near, d_cross, d_far = pl.pallas_call(
        functools.partial(attention_kernel, rows),
        grid=(kv_heads,),
        in_specs=[
            pl.BlockSpec(memory_space=pltpu.SMEM),
            heads,
            heads,
            cols(4),
            cols(4),
            cols(4),
            cols(4),
        ],
        out_specs=[heads, cols(2), cols(2), cols(4), cols(4), cols(4)],
        out_shape=[
            shape((rows, q_width), BF16),
            shape((2, rows, kv_width), F32),
            shape((2, rows, kv_width), F32),
            shape((4, rows, kv_width), F32),
            shape((4, rows, kv_width), BF16),
            shape((4, rows, kv_width), BF16),
        ],
        scratch_shapes=[
            pltpu.VMEM((GROUP * rows, HEAD_SIZE), BF16),
            pltpu.VMEM((GROUP * rows, HEAD_SIZE), BF16),
            pltpu.VMEM((window, HEAD_SIZE), BF16),
            pltpu.VMEM((window, HEAD_SIZE), BF16),
            pltpu.VMEM((HEAD_SIZE, window), BF16),
            pltpu.VMEM((window, rows), F32),
            pltpu.VMEM((window, 2 * rows), F32),
            pltpu.VMEM((window, 2 * rows), F32),
            pltpu.VMEM((window, GROUP * rows), BF16),
            pltpu.VMEM((window, GROUP * rows), BF16),
        ],
    )(doc_lengths, queries, d_out, full, near, cross, far)

    from_cross = permute(d_cross, devices, mate_of)
    from_far = permute_back(d_far, devices, far_of)
    near_sum = (d_near + from_cross.astype(F32)).astype(BF16)
    from_near = permute_back(near_sum, devices, near_of)
    arrived = from_near.astype(F32) + from_far.astype(F32)
    from_mate = permute((own_mate + arrived[2:]).astype(BF16), devices, mate_of)
    total = (own + arrived[:2] + from_mate.astype(F32)).astype(BF16)
    return d_queries, total[0], total[1]


def solution(mesh):
    spec = P(AXES, None)
    return jax.shard_map(
        local,
        mesh=mesh,
        in_specs=(spec, spec, spec, spec, P()),
        out_specs=(spec, spec, spec),
        check_vma=False,
    )
```

```python
import functools
import math

import jax
import jax.numpy as jnp
from jax import lax
from jax.experimental import pallas as pl
from jax.experimental.pallas import tpu as pltpu
from jax.sharding import PartitionSpec as P

HEAD_SIZE = 128
GROUP = 8
DOC_MOST = 768
AXES = ("dp", "seq")
SLOTS = 7
NEG = -1e30
VMEM_BYTES = 16 << 20
F32 = jnp.float32
BF16 = jnp.bfloat16


def weave(devices, turn):
    pairs = devices // 2
    moves, sources, targets = [], [], []
    taken = set()
    for c in range(pairs):
        back = -4 if c % 4 < 2 else -8
        if c % 2 == turn:
            steps = ((0, 1, 0), (1, 2, 0))
        else:
            steps = ((0, 3, 1), (1, back, 1))
        for core, step, target_core in steps:
            target = c + step
            if 0 <= target < pairs:
                moves.append((2 * c + core, 2 * target + target_core))
                taken.add(2 * target + target_core)
            else:
                sources.append(2 * c + core)
    targets = [d for d in range(devices) if d not in taken]
    rest = list(zip(sources, targets))
    for i, (source, target) in enumerate(rest):
        if source == target:
            j = i - 1 if i else 1
            rest[i], rest[j] = (source, rest[j][1]), (rest[j][0], target)
    return moves + rest


def swap(value, devices):
    return lax.ppermute(value, AXES, [(d, d ^ 1) for d in range(devices)])


def dot_nt(a, b):
    return lax.dot_general(a, b, (((1,), (1,)), ((), ())), preferred_element_type=F32)


def dot_nn(a, b):
    return lax.dot_general(a, b, (((1,), (0,)), ((), ())), preferred_element_type=F32)


def attention_kernel(
    rows,
    lens_ref,
    q_ref,
    g_ref,
    full_ref,
    a_ref,
    ax_ref,
    b_ref,
    bx_ref,
    dq_ref,
    own_ref,
    mate_ref,
    keep2_ref,
    keep1_ref,
    give2_ref,
    give1_ref,
    qs,
    gs,
    kwin,
    vwin,
    kt,
    bias,
    sc,
    gp,
    pt,
    dst,
):
    t = rows
    scale = 1.0 / math.sqrt(HEAD_SIZE)
    scale2 = scale * math.log2(math.e)
    me = lax.axis_index("dp") * lax.axis_size("seq") + lax.axis_index("seq")
    odd = lax.rem(me, 2) == 1
    odd_pair = lax.rem(me // 2, 2) == 1
    first = me * t
    q_pos = first + lax.broadcasted_iota(jnp.int32, (1, t), 1)

    def next_doc(j, carry):
        end, low = carry
        end = end + lens_ref[j]
        return end, jnp.where(end <= q_pos, end, low)

    _, low = lax.fori_loop(
        0, lens_ref.shape[0], next_doc, (jnp.int32(0), jnp.zeros((1, t), jnp.int32))
    )
    for slot, (even_back, odd_back) in enumerate(
        ((0, 0), (6, 1), (2, 3), (1, 2), (4, 5), (3, 4), (5, 6))
    ):
        back = jnp.where(odd, odd_back, even_back)
        k_pos = first - back * t + lax.broadcasted_iota(jnp.int32, (t, t), 0)
        allowed = k_pos >= low
        if slot == 0:
            allowed = allowed & (k_pos <= q_pos)
        bias[slot * t : (slot + 1) * t, :] = jnp.where(allowed, 0.0, NEG)

    for head in range(full_ref.shape[2] // HEAD_SIZE):
        lanes = slice(head * HEAD_SIZE, (head + 1) * HEAD_SIZE)

        def q_lanes(h, head=head):
            at = (head * GROUP + h) * HEAD_SIZE
            return slice(at, at + HEAD_SIZE)

        for h in range(GROUP):
            qs[h * t : (h + 1) * t, :] = q_ref[:, q_lanes(h)]
            gs[h * t : (h + 1) * t, :] = g_ref[:, q_lanes(h)]

        def fill(core, one, two, three, lanes=lanes):
            chosen = (
                (full_ref, 2 * core),
                (full_ref, 0) if core else (three, 0),
                (one, 0),
                (one, 2),
                (two, 0),
                (two, 2),
                (three, 2),
            )
            for slot, (ref, at) in enumerate(chosen):
                span = slice(slot * t, (slot + 1) * t)
                kwin[span, :] = ref[at, :, lanes]
                vwin[span, :] = ref[at + 1, :, lanes]

        for pair_parity in (0, 1):
            for core in (0, 1):
                two_at, one_at = ((a_ref, ax_ref), (b_ref, bx_ref))
                if pair_parity:
                    two_at, one_at = one_at, two_at
                one, two, three = one_at[core], two_at[core], two_at[1 - core]

                @pl.when((odd_pair == bool(pair_parity)) & (odd == bool(core)))
                def _(core=core, one=one, two=two, three=three):
                    fill(core, one, two, three)

        for slot in range(SLOTS):
            span = slice(slot * t, (slot + 1) * t)
            kt[:, span] = kwin[span, :].T

        for pair in range(GROUP // 2):
            cols = slice(pair * 2 * t, (pair + 1) * 2 * t)
            sc[...] = dot_nt(kwin[...], qs[cols, :])
            gp[...] = dot_nt(vwin[...], gs[cols, :])
            top = None
            for slot in range(SLOTS):
                span = slice(slot * t, (slot + 1) * t)
                b = bias[span, :]
                s = sc[span, :] * scale2 + jnp.concatenate([b, b], axis=1)
                sc[span, :] = s
                high = jnp.max(s, axis=0, keepdims=True)
                top = high if top is None else jnp.maximum(top, high)
            total = jnp.zeros((1, 2 * t), F32)
            weighted = jnp.zeros((1, 2 * t), F32)
            for slot in range(SLOTS):
                span = slice(slot * t, (slot + 1) * t)
                e = jnp.exp2(sc[span, :] - top)
                sc[span, :] = e
                total += jnp.sum(e, axis=0, keepdims=True)
                weighted += jnp.sum(e * gp[span, :], axis=0, keepdims=True)
            inverse = 1.0 / total
            delta = weighted * inverse
            for slot in range(SLOTS):
                span = slice(slot * t, (slot + 1) * t)
                p = sc[span, :] * inverse
                ds = p * (gp[span, :] - delta) * scale
                pt[span, cols] = p.astype(BF16)
                dst[span, cols] = ds.astype(BF16)

        dk = dot_nn(dst[...], qs[...])
        dv = dot_nn(pt[...], gs[...])

        def part(grad, slot):
            return grad[slot * t : (slot + 1) * t, :]

        none = jnp.zeros((t, HEAD_SIZE), F32)
        for kind, grad in enumerate((dk, dv)):
            own_ref[kind, :, lanes] = part(grad, 0)
            mate_ref[kind, :, lanes] = jnp.where(odd, part(grad, 1), none)
            third_even = jnp.where(odd, none, part(grad, 1))
            two, three = (part(grad, 4), part(grad, 5)), (third_even, part(grad, 6))
            one = (part(grad, 2), part(grad, 3))
            for side in (0, 1):
                at = kind + 2 * side
                give2_ref[at, :, lanes] = jnp.where(odd, two[side], three[side]).astype(BF16)
                give1_ref[at, :, lanes] = one[side].astype(BF16)
                keep2_ref[at, :, lanes] = jnp.where(odd, three[side], two[side]).astype(BF16)
                keep1_ref[at, :, lanes] = jnp.where(odd, none, one[side]).astype(BF16)
        dqt = dot_nn(kt[...], dst[...])
        for h in range(GROUP):
            dq_ref[:, q_lanes(h)] = dqt[:, h * t : (h + 1) * t].T.astype(BF16)


def local(queries, keys, values, d_out, doc_lengths):
    rows, q_width = queries.shape
    kv_width = keys.shape[1]
    devices = lax.axis_size("dp") * lax.axis_size("seq")
    me = lax.axis_index("dp") * lax.axis_size("seq") + lax.axis_index("seq")
    odd = lax.rem(me, 2) == 1
    odd_pair = lax.rem(me // 2, 2) == 1
    a_moves, b_moves = weave(devices, 0), weave(devices, 1)

    mate_k, mate_v = swap(keys, devices), swap(values, devices)
    mine, mate = jnp.stack([keys, values]), jnp.stack([mate_k, mate_v])
    full = jnp.concatenate([jnp.where(odd, mate, mine), jnp.where(odd, mine, mate)], axis=0)
    a = lax.ppermute(full, AXES, a_moves)
    b = lax.ppermute(full, AXES, b_moves)
    ax, bx = swap(a, devices), swap(b, devices)

    window = SLOTS * rows
    shape = jax.ShapeDtypeStruct
    in_vmem = pl.BlockSpec(memory_space=pltpu.VMEM)
    piece = shape((4, rows, kv_width), BF16)
    d_queries, own, own_mate, keep2, keep1, give2, give1 = pl.pallas_call(
        functools.partial(attention_kernel, rows),
        in_specs=[pl.BlockSpec(memory_space=pltpu.SMEM)] + [in_vmem] * 7,
        out_specs=[in_vmem] * 7,
        out_shape=[
            shape((rows, q_width), BF16),
            shape((2, rows, kv_width), F32),
            shape((2, rows, kv_width), F32),
            piece,
            piece,
            piece,
            piece,
        ],
        scratch_shapes=[
            pltpu.VMEM((GROUP * rows, HEAD_SIZE), BF16),
            pltpu.VMEM((GROUP * rows, HEAD_SIZE), BF16),
            pltpu.VMEM((window, HEAD_SIZE), BF16),
            pltpu.VMEM((window, HEAD_SIZE), BF16),
            pltpu.VMEM((HEAD_SIZE, window), BF16),
            pltpu.VMEM((window, rows), F32),
            pltpu.VMEM((window, 2 * rows), F32),
            pltpu.VMEM((window, 2 * rows), F32),
            pltpu.VMEM((window, GROUP * rows), BF16),
            pltpu.VMEM((window, GROUP * rows), BF16),
        ],
        compiler_params=pltpu.CompilerParams(vmem_limit_bytes=VMEM_BYTES),
    )(doc_lengths, queries, d_out, full, a, ax, b, bx)

    got2, got1 = swap(give2, devices), swap(give1, devices)
    back2 = (keep2.astype(F32) + got2.astype(F32)).astype(BF16)
    back1 = jnp.where(odd, jnp.zeros_like(keep1), (keep1.astype(F32) + got1.astype(F32)).astype(BF16))
    home_a = lax.ppermute(jnp.where(odd_pair, back1, back2), AXES, [(d, s) for s, d in a_moves])
    home_b = lax.ppermute(jnp.where(odd_pair, back2, back1), AXES, [(d, s) for s, d in b_moves])
    arrived = home_a.astype(F32) + home_b.astype(F32)
    mine_in = jnp.where(odd, arrived[2:], arrived[:2])
    mate_in = jnp.where(odd, arrived[:2], arrived[2:])
    from_mate = swap((own_mate + mate_in).astype(BF16), devices)
    total = (own + mine_in + from_mate.astype(F32)).astype(BF16)
    return d_queries, total[0], total[1]


def solution(mesh):
    spec = P(AXES, None)
    return jax.shard_map(
        local,
        mesh=mesh,
        in_specs=(spec, spec, spec, spec, P()),
        out_specs=(spec, spec, spec),
        check_vma=False,
    )
```

```python
import functools
import math

import jax
import jax.numpy as jnp
from jax import lax
from jax.experimental import pallas as pl
from jax.experimental.pallas import tpu as pltpu
from jax.sharding import PartitionSpec as P

HEAD_SIZE = 128
GROUP = 8
AXES = ("dp", "seq")
SLOTS = 7
NEG = -1e30
FAR = 1 << 30
WINDOW_BACK = ((0, 0), (6, 1), (2, 3), (1, 2), (4, 5), (3, 4), (5, 6))
F32 = jnp.float32
BF16 = jnp.bfloat16


def weave(devices, turn):
    pairs = devices // 2
    moves, sources, targets = [], [], []
    taken = set()
    for c in range(pairs):
        back = -4 if c % 4 < 2 else -8
        if c % 2 == turn:
            steps = ((0, 1, 0), (1, 2, 0))
        else:
            steps = ((0, 3, 1), (1, back, 1))
        for core, step, target_core in steps:
            target = c + step
            if 0 <= target < pairs:
                moves.append((2 * c + core, 2 * target + target_core))
                taken.add(2 * target + target_core)
            else:
                sources.append(2 * c + core)
    targets = [d for d in range(devices) if d not in taken]
    rest = list(zip(sources, targets))
    for i, (source, target) in enumerate(rest):
        if source == target:
            j = i - 1 if i else 1
            rest[i], rest[j] = (source, rest[j][1]), (rest[j][0], target)
    return moves + rest


def swap(value, devices):
    return lax.ppermute(value, AXES, [(d, d ^ 1) for d in range(devices)])


def dot_nt(a, b):
    return lax.dot_general(a, b, (((1,), (1,)), ((), ())), preferred_element_type=F32)


def dot_nn(a, b):
    return lax.dot_general(a, b, (((1,), (0,)), ((), ())), preferred_element_type=F32)


def prepare_kernel(rows, window_back, lens_ref, q_ref, g_ref, qa_ref, gs_ref, late_ref, sems):
    t = rows
    copies = []
    for h in range(q_ref.shape[1] // HEAD_SIZE):
        span, lanes = slice(h * t, (h + 1) * t), slice(h * HEAD_SIZE, (h + 1) * HEAD_SIZE)
        for source, target, sem in (
            (q_ref.at[:, lanes], qa_ref.at[span, :HEAD_SIZE], sems.at[0, h]),
            (g_ref.at[:, lanes], gs_ref.at[span, :], sems.at[1, h]),
        ):
            copies.append(pltpu.make_async_copy(source, target, sem))
    for copy in copies:
        copy.start()
    me = lax.axis_index("dp") * lax.axis_size("seq") + lax.axis_index("seq")
    odd = lax.rem(me, 2) == 1
    first = me * t
    lane = lax.broadcasted_iota(jnp.int32, (1, HEAD_SIZE), 1)

    def next_doc(j, carry):
        end, count, starts, stops = carry
        begin, end = end, end + lens_ref[j]
        live = end > first
        here = (lane == count) & live
        starts, stops = jnp.where(here, begin, starts), jnp.where(here, end, stops)
        return end, count + live.astype(jnp.int32), starts, stops

    far = jnp.full((1, HEAD_SIZE), FAR, jnp.int32)
    zero = jnp.int32(0)
    _, _, starts, stops = lax.fori_loop(0, lens_ref.shape[0], next_doc, (zero, zero, far, far))
    down = lax.broadcasted_iota(jnp.int32, (t, HEAD_SIZE), 0)
    q_pos = first + down
    member = jnp.where((q_pos >= starts) & (q_pos < stops), 1.0, 0.0).astype(BF16)
    for slot, (even_back, odd_back) in enumerate(window_back):
        k_pos = first - jnp.where(odd, odd_back, even_back) * t + down
        late_ref[slot * t : (slot + 1) * t, :] = jnp.where(k_pos < starts, NEG, 0.0).astype(BF16)
    for h in range(q_ref.shape[1] // HEAD_SIZE):
        qa_ref[h * t : (h + 1) * t, HEAD_SIZE:] = member
    for copy in copies:
        copy.wait()


def attention_kernel(
    rows,
    qa_ref,
    gs_ref,
    late_ref,
    full_ref,
    a_ref,
    ax_ref,
    b_ref,
    bx_ref,
    own_ref,
    mate_ref,
    keep2_ref,
    keep1_ref,
    give2_ref,
    give1_ref,
    ka_ref,
    dst_ref,
    vwin,
    sc,
    gp,
    pt,
):
    t = rows
    scale = 1.0 / math.sqrt(HEAD_SIZE)
    scale2 = scale * math.log2(math.e)
    me = lax.axis_index("dp") * lax.axis_size("seq") + lax.axis_index("seq")
    odd = lax.rem(me, 2) == 1
    odd_pair = lax.rem(me // 2, 2) == 1
    causal = lax.broadcasted_iota(jnp.int32, (t, t), 0) <= lax.broadcasted_iota(
        jnp.int32, (t, t), 1
    )
    causal = jnp.concatenate([causal, causal], axis=1)

    def spans():
        return [slice(slot * t, (slot + 1) * t) for slot in range(SLOTS)]

    def fold(x, op):
        return op(x.reshape(t // 8, 8, 2 * t), axis=0)

    for head in range(full_ref.shape[2] // HEAD_SIZE):
        lanes = slice(head * HEAD_SIZE, (head + 1) * HEAD_SIZE)
        base = head * GROUP * t

        def fill(core, one, two, three, head=head, lanes=lanes):
            chosen = (
                (full_ref, 2 * core),
                (full_ref, 0) if core else (three, 0),
                (one, 0),
                (one, 2),
                (two, 0),
                (two, 2),
                (three, 2),
            )
            for span, (ref, at) in zip(spans(), chosen):
                ka_ref[head, span, :HEAD_SIZE] = ref[at, :, lanes]
                vwin[span, :] = ref[at + 1, :, lanes]

        for pair_parity in (0, 1):
            for core in (0, 1):
                two_at, one_at = ((a_ref, ax_ref), (b_ref, bx_ref))
                if pair_parity:
                    two_at, one_at = one_at, two_at
                one, two, three = one_at[core], two_at[core], two_at[1 - core]

                @pl.when((odd_pair == bool(pair_parity)) & (odd == bool(core)))
                def _(core=core, one=one, two=two, three=three):
                    fill(core, one, two, three)

        ka_ref[head, :, HEAD_SIZE:] = late_ref[...]

        for pair in range(GROUP // 2):
            cols = slice(pair * 2 * t, (pair + 1) * 2 * t)
            pair_rows = slice(base + pair * 2 * t, base + (pair + 1) * 2 * t)
            sc[...] = dot_nt(ka_ref[head], qa_ref[pair_rows, :])
            gp[...] = dot_nt(vwin[...], gs_ref[pair_rows, :])
            top = None
            for slot, span in enumerate(spans()):
                s = sc[span, :] * scale2
                if slot == 0:
                    s = jnp.where(causal, s, NEG)
                sc[span, :] = s
                high = fold(s, jnp.max)
                top = high if top is None else jnp.maximum(top, high)
            top = jnp.max(top, axis=0, keepdims=True)
            total = jnp.zeros((8, 2 * t), F32)
            weighted = jnp.zeros((8, 2 * t), F32)
            for span in spans():
                e = jnp.exp2(sc[span, :] - top)
                total += fold(e, jnp.sum)
                weighted += fold(e * gp[span, :], jnp.sum)
            total = jnp.sum(total, axis=0, keepdims=True)
            delta = jnp.sum(weighted, axis=0, keepdims=True) / total
            level = top + jnp.log2(total)
            for span in spans():
                p = jnp.exp2(sc[span, :] - level)
                pt[span, cols] = p.astype(BF16)
                dst_ref[head, span, cols] = (p * (gp[span, :] - delta)).astype(BF16)

        all_rows = slice(base, base + GROUP * t)
        dk = dot_nn(dst_ref[head], qa_ref[all_rows, :HEAD_SIZE]) * scale
        dv = dot_nn(pt[...], gs_ref[all_rows, :])

        def part(grad, slot):
            return grad[slot * t : (slot + 1) * t, :]

        none = jnp.zeros((t, HEAD_SIZE), F32)
        for kind, grad in enumerate((dk, dv)):
            own_ref[kind, :, lanes] = part(grad, 0)
            mate_ref[kind, :, lanes] = jnp.where(odd, part(grad, 1), none)
            third_even = jnp.where(odd, none, part(grad, 1))
            two, three = (part(grad, 4), part(grad, 5)), (third_even, part(grad, 6))
            one = (part(grad, 2), part(grad, 3))
            for side in (0, 1):
                at = kind + 2 * side
                give2_ref[at, :, lanes] = jnp.where(odd, two[side], three[side]).astype(BF16)
                give1_ref[at, :, lanes] = one[side].astype(BF16)
                keep2_ref[at, :, lanes] = jnp.where(odd, three[side], two[side]).astype(BF16)
                keep1_ref[at, :, lanes] = jnp.where(odd, none, one[side]).astype(BF16)


def query_kernel(rows, ka_ref, dst_ref, dq_ref, kt):
    t = rows
    scale = 1.0 / math.sqrt(HEAD_SIZE)
    for head in range(ka_ref.shape[0]):
        for slot in range(SLOTS):
            span = slice(slot * t, (slot + 1) * t)
            kt[:, span] = ka_ref[head, span, :HEAD_SIZE].T
        dqt = dot_nn(kt[...], dst_ref[head]) * scale
        for h in range(GROUP):
            at = (head * GROUP + h) * HEAD_SIZE
            dq_ref[:, at : at + HEAD_SIZE] = dqt[:, h * t : (h + 1) * t].T.astype(BF16)


def local_grads(queries, keys, values, d_out, doc_lengths):
    rows, q_width = queries.shape
    kv_width = keys.shape[1]
    devices = lax.axis_size("dp") * lax.axis_size("seq")
    me = lax.axis_index("dp") * lax.axis_size("seq") + lax.axis_index("seq")
    odd = lax.rem(me, 2) == 1
    odd_pair = lax.rem(me // 2, 2) == 1
    a_moves, b_moves = weave(devices, 0), weave(devices, 1)

    mine = lax.optimization_barrier(jnp.stack([keys, values]))
    mate = swap(mine, devices)
    full = jnp.concatenate([jnp.where(odd, mate, mine), jnp.where(odd, mine, mate)], axis=0)
    a = lax.ppermute(full, AXES, a_moves)
    b = lax.ppermute(full, AXES, b_moves)
    ax, bx = swap(a, devices), swap(b, devices)

    window = SLOTS * rows
    kv_heads = kv_width // HEAD_SIZE
    tall = q_width // HEAD_SIZE * rows
    shape = jax.ShapeDtypeStruct
    in_vmem = pl.BlockSpec(memory_space=pltpu.VMEM)
    piece = shape((4, rows, kv_width), BF16)
    grant = pltpu.CompilerParams(vmem_limit_bytes=(12 + 5 * kv_heads) << 20)
    qa, gs, late = pl.pallas_call(
        functools.partial(prepare_kernel, rows, WINDOW_BACK),
        in_specs=[pl.BlockSpec(memory_space=pltpu.SMEM)] + [pl.BlockSpec(memory_space=pl.ANY)] * 2,
        out_specs=[in_vmem] * 3,
        out_shape=[
            shape((tall, 2 * HEAD_SIZE), BF16),
            shape((tall, HEAD_SIZE), BF16),
            shape((window, HEAD_SIZE), BF16),
        ],
        scratch_shapes=[pltpu.SemaphoreType.DMA((2, q_width // HEAD_SIZE))],
        compiler_params=grant,
        cost_estimate=pl.CostEstimate(flops=0, bytes_accessed=4 << 20, transcendentals=0),
    )(doc_lengths, queries, d_out)
    own, own_mate, keep2, keep1, give2, give1, ka, dst = pl.pallas_call(
        functools.partial(attention_kernel, rows),
        in_specs=[in_vmem] * 8,
        out_specs=[in_vmem] * 8,
        out_shape=[
            shape((2, rows, kv_width), F32),
            shape((2, rows, kv_width), F32),
            piece,
            piece,
            piece,
            piece,
            shape((kv_heads, window, 2 * HEAD_SIZE), BF16),
            shape((kv_heads, window, GROUP * rows), BF16),
        ],
        scratch_shapes=[
            pltpu.VMEM((window, HEAD_SIZE), BF16),
            pltpu.VMEM((window, 2 * rows), F32),
            pltpu.VMEM((window, 2 * rows), F32),
            pltpu.VMEM((window, GROUP * rows), BF16),
        ],
        compiler_params=grant,
    )(qa, gs, late, full, a, ax, b, bx)
    d_queries = pl.pallas_call(
        functools.partial(query_kernel, rows),
        in_specs=[in_vmem] * 2,
        out_specs=in_vmem,
        out_shape=shape((rows, q_width), BF16),
        scratch_shapes=[pltpu.VMEM((HEAD_SIZE, window), BF16)],
        compiler_params=grant,
        cost_estimate=pl.CostEstimate(flops=1 << 28, bytes_accessed=4 << 20, transcendentals=0),
    )(ka, dst)

    got2, got1 = swap(give2, devices), swap(give1, devices)
    back2 = (keep2.astype(F32) + got2.astype(F32)).astype(BF16)
    back1 = jnp.where(odd, jnp.zeros_like(keep1), (keep1.astype(F32) + got1.astype(F32)).astype(BF16))
    home_a = lax.ppermute(jnp.where(odd_pair, back1, back2), AXES, [(d, s) for s, d in a_moves])
    home_b = lax.ppermute(jnp.where(odd_pair, back2, back1), AXES, [(d, s) for s, d in b_moves])
    arrived = home_a.astype(F32) + home_b.astype(F32)
    mine_in = jnp.where(odd, arrived[2:], arrived[:2])
    mate_in = jnp.where(odd, arrived[:2], arrived[2:])
    from_mate = swap((own_mate + mate_in).astype(BF16), devices)
    total = (own + mine_in + from_mate.astype(F32)).astype(BF16)
    return d_queries, total[0], total[1]


def solution(mesh):
    spec = P(AXES, None)
    return jax.shard_map(
        local_grads,
        mesh=mesh,
        in_specs=(spec, spec, spec, spec, P()),
        out_specs=(spec, spec, spec),
        check_vma=False,
    )
```

```python
import functools
import math

import jax
import jax.numpy as jnp
from jax import lax
from jax.experimental import pallas as pl
from jax.experimental.pallas import tpu as pltpu
from jax.sharding import PartitionSpec as P

HEAD_SIZE = 128
GROUP = 8
AXES = ("dp", "seq")
NEG = -1e30
FAR = 1 << 30
SCALE = 1.0 / math.sqrt(HEAD_SIZE)
SCALE2 = SCALE * math.log2(math.e)
F32 = jnp.float32
BF16 = jnp.bfloat16


def weave(devices, turn):
    pairs = devices // 2
    moves, sources, taken = [], [], set()
    for c in range(pairs):
        back = -4 if c % 4 < 2 else -8
        if c % 2 == turn:
            steps = ((0, 1, 0), (1, 2, 0))
        else:
            steps = ((0, 3, 1), (1, back, 1))
        for core, step, target_core in steps:
            target = c + step
            if 0 <= target < pairs:
                moves.append((2 * c + core, 2 * target + target_core))
                taken.add(2 * target + target_core)
            else:
                sources.append(2 * c + core)
    targets = [d for d in range(devices) if d not in taken]
    rest = list(zip(sources, targets))
    for i, (source, target) in enumerate(rest):
        if source == target:
            j = i - 1 if i else 1
            rest[i], rest[j] = (source, rest[j][1]), (rest[j][0], target)
    return moves + rest


def swap(value, devices):
    return lax.ppermute(value, AXES, [(d, d ^ 1) for d in range(devices)])


def dot_nt(a, b):
    return lax.dot_general(a, b, (((1,), (1,)), ((), ())), preferred_element_type=F32)


def dot_nn(a, b):
    return lax.dot_general(a, b, (((1,), (0,)), ((), ())), preferred_element_type=F32)


def where_am_i():
    me = lax.axis_index("dp") * lax.axis_size("seq") + lax.axis_index("seq")
    return me, lax.rem(me, 2) == 1, lax.rem(me // 2, 2) == 1


def holds_own(block, odd, odd_pair):
    return odd & (odd_pair if block else jnp.logical_not(odd_pair))


def prepare_kernel(
    rows, lens_hbm, q_hbm, g_hbm, q_ref, g_ref, member_ref, late_ref, lens_ref, lens_sem, q_sem, g_sem
):
    t = rows
    fetch = pltpu.make_async_copy(lens_hbm, lens_ref, lens_sem)
    fetch_q = pltpu.make_async_copy(q_hbm, q_ref, q_sem)
    fetch_g = pltpu.make_async_copy(g_hbm, g_ref, g_sem)
    fetch.start()
    fetch_q.start()
    fetch_g.start()
    me, odd, odd_pair = where_am_i()
    lane = lax.broadcasted_iota(jnp.int32, (1, HEAD_SIZE), 1)
    down = lax.broadcasted_iota(jnp.int32, (t, HEAD_SIZE), 0)
    pair_first = (me // 2) * 2 * t
    far = jnp.full((1, HEAD_SIZE), FAR, jnp.int32)
    zero = jnp.int32(0)
    fetch.wait()
    for side in (0, 1):
        first = (me if side == 0 else jnp.where(odd, me - 1, me + 1)) * t

        def next_doc(j, carry, first=first):
            end, count, starts, stops = carry
            begin, end = end, end + lens_ref[j]
            live = end > first
            here = (lane == count) & live
            starts, stops = jnp.where(here, begin, starts), jnp.where(here, end, stops)
            return end, count + live.astype(jnp.int32), starts, stops

        _, _, starts, stops = lax.fori_loop(0, lens_ref.shape[0], next_doc, (zero, zero, far, far))
        q_pos = first + down
        member = jnp.where((q_pos >= starts) & (q_pos < stops), 1.0, 0.0).astype(BF16)
        member_ref[side, :t, :] = member
        member_ref[side, t:, :] = member
        for block in (0, 1):
            one_back = jnp.where(odd, 0, -1)
            far_back = jnp.where(odd, -3, -2)
            single = odd_pair if block else jnp.logical_not(odd_pair)
            base = pair_first + jnp.where(single, one_back, far_back) * 2 * t
            for part in (0, 1):
                k_pos = base + part * t + down
                blocked = (k_pos < starts) | (k_pos >= first + t)
                late_ref[block, side, part * t : (part + 1) * t, :] = jnp.where(
                    blocked, NEG, 0.0
                ).astype(BF16)
    fetch_q.wait()
    fetch_g.wait()


def stacked(ref, first_head, count):
    return jnp.concatenate(
        [ref[:, h * HEAD_SIZE : (h + 1) * HEAD_SIZE] for h in range(first_head, first_head + count)],
        axis=0,
    )


def combine(one, two):
    high = jnp.maximum(one[0], two[0])
    keep_one, keep_two = jnp.exp2(one[0] - high), jnp.exp2(two[0] - high)
    return high, one[1] * keep_one + two[1] * keep_two, one[2] * keep_one + two[2] * keep_two


def score_kernel(rows, block, *refs):
    qs, gs = (refs[0], refs[2]), (refs[1], refs[3])
    member_ref, late_ref, full_ref, got_ref = refs[4:8]
    before_ref = refs[8] if block else None
    s_ref, g_ref, stats_ref = refs[-3:]
    t = rows
    _, odd, odd_pair = where_am_i()
    own = holds_own(block, odd, odd_pair)
    reach = jnp.where(own, 0, FAR)
    down = lax.broadcasted_iota(jnp.int32, (t, t), 0)
    across = lax.broadcasted_iota(jnp.int32, (t, t), 1)
    causal = down - across <= reach
    causal = jnp.concatenate([causal, causal], axis=1)

    def fold(x, op):
        return op(x.reshape(-1, 8, 2 * t), axis=0)

    for head in range(full_ref.shape[2] // HEAD_SIZE):
        lanes = slice(head * HEAD_SIZE, (head + 1) * HEAD_SIZE)
        key, value = (jnp.where(own, full_ref[i, :, lanes], got_ref[i, :, lanes]) for i in (0, 1))
        for side in (0, 1):
            key_late = jnp.concatenate([key, late_ref[block, side]], axis=1)
            for pair in range(GROUP // 2):
                cols = slice((side * GROUP + pair * 2) * t, (side * GROUP + pair * 2 + 2) * t)
                q_rows = stacked(qs[side], head * GROUP + pair * 2, 2)
                q_rows = jnp.concatenate([q_rows, member_ref[side]], axis=1)
                s = dot_nt(key_late, q_rows) * SCALE2
                g = dot_nt(value, stacked(gs[side], head * GROUP + pair * 2, 2))
                parts = [s[:t], s[t:]]
                parts[1 - side] = jnp.where(causal, parts[1 - side], NEG)
                s_ref[head, :t, cols] = parts[0]
                s_ref[head, t:, cols] = parts[1]
                g_ref[head, :, cols] = g
                top = jnp.maximum(fold(parts[0], jnp.max), fold(parts[1], jnp.max))
                top = jnp.max(top, axis=0, keepdims=True)
                total = jnp.zeros((8, 2 * t), F32)
                weighted = jnp.zeros((8, 2 * t), F32)
                for part in (0, 1):
                    e = jnp.exp2(parts[part] - top)
                    total += fold(e, jnp.sum)
                    weighted += fold(e * g[part * t : (part + 1) * t], jnp.sum)
                found = (
                    top,
                    jnp.sum(total, axis=0, keepdims=True),
                    jnp.sum(weighted, axis=0, keepdims=True),
                )
                if block:
                    found = combine(
                        found, [before_ref[3 * head + i : 3 * head + i + 1, cols] for i in range(3)]
                    )
                for i in range(3):
                    stats_ref[3 * head + i : 3 * head + i + 1, cols] = found[i]


def grads_kernel(rows, block, *refs):
    qs, gs = (refs[0], refs[2]), (refs[1], refs[3])
    s_ref, g_ref, stats_ref, other_ref, home_ref, own_ref, ds_ref, pt = refs[4:]
    t = rows
    _, odd, odd_pair = where_am_i()
    own = holds_own(block, odd, odd_pair)
    for head in range(s_ref.shape[0]):
        lanes = slice(head * HEAD_SIZE, (head + 1) * HEAD_SIZE)
        grads = [None, None]
        for side in (0, 1):
            for pair in range(GROUP // 2):
                cols = slice((side * GROUP + pair * 2) * t, (side * GROUP + pair * 2 + 2) * t)
                turned = slice(
                    ((1 - side) * GROUP + pair * 2) * t, ((1 - side) * GROUP + pair * 2 + 2) * t
                )
                high, total, weighted = combine(
                    [stats_ref[3 * head + i : 3 * head + i + 1, cols] for i in range(3)],
                    [other_ref[3 * head + i : 3 * head + i + 1, turned] for i in range(3)],
                )
                level, delta = high + jnp.log2(total), weighted / total
                p = jnp.exp2(s_ref[head, :, cols] - level)
                pt[:, cols] = p.astype(BF16)
                ds_ref[head, :, cols] = (p * (g_ref[head, :, cols] - delta)).astype(BF16)
            cols = slice(side * GROUP * t, (side + 1) * GROUP * t)
            dk = dot_nn(ds_ref[head, :, cols], stacked(qs[side], head * GROUP, GROUP)) * SCALE
            dv = dot_nn(pt[:, cols], stacked(gs[side], head * GROUP, GROUP))
            grads = [dk, dv] if side == 0 else [grads[0] + dk, grads[1] + dv]
        for kind, grad in enumerate(grads):
            none = jnp.zeros_like(grad)
            home_ref[kind, :, lanes] = jnp.where(own, none, grad).astype(BF16)
            own_ref[kind, :, lanes] = jnp.where(own, grad, none)


def query_kernel(rows, full_ref, b_ref, a_ref, dsb_ref, dsa_ref, mine_ref, mate_ref):
    t = rows
    _, odd, odd_pair = where_am_i()
    for head in range(dsb_ref.shape[0]):
        lanes = slice(head * HEAD_SIZE, (head + 1) * HEAD_SIZE)
        key_b, key_a = (
            jnp.where(holds_own(block, odd, odd_pair), full_ref[0, :, lanes], got[0, :, lanes]).T
            for block, got in ((0, b_ref), (1, a_ref))
        )
        for side, out_ref in ((1, mate_ref), (0, mine_ref)):
            cols = slice(side * GROUP * t, (side + 1) * GROUP * t)
            dqt = dot_nn(key_b, dsb_ref[head, :, cols]) + dot_nn(key_a, dsa_ref[head, :, cols])
            dqt = dqt * SCALE
            for h in range(GROUP):
                at = (head * GROUP + h) * HEAD_SIZE
                out_ref[:, at : at + HEAD_SIZE] = dqt[:, h * t : (h + 1) * t].T.astype(out_ref.dtype)


def local_grads(queries, keys, values, d_out, doc_lengths):
    rows, q_width = queries.shape
    kv_width = keys.shape[1]
    kv_heads = kv_width // HEAD_SIZE
    devices = lax.axis_size("dp") * lax.axis_size("seq")
    _, odd, _ = where_am_i()
    a_moves, b_moves = weave(devices, 0), weave(devices, 1)

    mine = lax.optimization_barrier(jnp.stack([keys, values]))
    mate_k, mate_v = swap(keys, devices), swap(values, devices)
    mate = jnp.stack([mate_k, mate_v])
    full = jnp.concatenate([jnp.where(odd, mate, mine), jnp.where(odd, mine, mate)], axis=1)
    full = lax.optimization_barrier(full)
    b = lax.ppermute(full, AXES, b_moves)
    a = lax.ppermute(full, AXES, a_moves)
    mate_q = swap(queries, devices)
    mate_g = swap(d_out, devices)

    shape = jax.ShapeDtypeStruct
    in_vmem = pl.BlockSpec(memory_space=pltpu.VMEM)
    grant = pltpu.CompilerParams(vmem_limit_bytes=(12 + 10 * kv_heads) << 20)

    def cost(flops):
        return pl.CostEstimate(flops=flops, bytes_accessed=1 << 20, transcendentals=0)

    width = 2 * GROUP * rows
    mine_q, mine_g, member, late = pl.pallas_call(
        functools.partial(prepare_kernel, rows),
        in_specs=[pl.BlockSpec(memory_space=pltpu.HBM)] * 3,
        out_specs=[in_vmem] * 4,
        out_shape=[
            shape((rows, q_width), BF16),
            shape((rows, q_width), BF16),
            shape((2, 2 * rows, HEAD_SIZE), BF16),
            shape((2, 2, 2 * rows, HEAD_SIZE), BF16),
        ],
        scratch_shapes=[
            pltpu.SMEM(doc_lengths.shape, jnp.int32),
            pltpu.SemaphoreType.DMA,
            pltpu.SemaphoreType.DMA,
            pltpu.SemaphoreType.DMA,
        ],
        compiler_params=grant,
        cost_estimate=cost(1 << 20),
    )(doc_lengths, queries, d_out)

    rows_of = (mine_q, mine_g, mate_q, mate_g)

    def scores(block, got, *before):
        return pl.pallas_call(
            functools.partial(score_kernel, rows, block),
            in_specs=[in_vmem] * (8 + len(before)),
            out_specs=[in_vmem] * 3,
            out_shape=[
                shape((kv_heads, 2 * rows, width), F32),
                shape((kv_heads, 2 * rows, width), F32),
                shape((3 * kv_heads, width), F32),
            ],
            compiler_params=grant,
            cost_estimate=cost(1 << 28),
        )(*rows_of, member, late, full, got, *before)

    def grads(block, s, g, stats, other):
        return pl.pallas_call(
            functools.partial(grads_kernel, rows, block),
            in_specs=[in_vmem] * 8,
            out_specs=[in_vmem] * 3,
            out_shape=[
                shape((2, 2 * rows, kv_width), BF16),
                shape((2, 2 * rows, kv_width), F32),
                shape((kv_heads, 2 * rows, width), BF16),
            ],
            scratch_shapes=[pltpu.VMEM((2 * rows, width), BF16)],
            compiler_params=grant,
            cost_estimate=cost(1 << 28),
        )(*rows_of, s, g, stats, other)

    s_b, g_b, stats_b = scores(0, b)
    s_a, g_a, stats = scores(1, a, stats_b)
    other = swap(stats, devices)
    back_b, own_b, ds_b = grads(0, s_b, g_b, stats, other)
    home_b = lax.ppermute(back_b, AXES, [(d, s) for s, d in b_moves])
    back_a, own_a, ds_a = grads(1, s_a, g_a, stats, other)
    home_a = lax.ppermute(back_a, AXES, [(d, s) for s, d in a_moves])
    dq_mine, dq_mate = pl.pallas_call(
        functools.partial(query_kernel, rows),
        in_specs=[in_vmem] * 5,
        out_specs=[in_vmem] * 2,
        out_shape=[shape((rows, q_width), F32), shape((rows, q_width), BF16)],
        compiler_params=grant,
        cost_estimate=cost(1 << 28),
    )(full, b, a, ds_b, ds_a)
    dq_other = swap(dq_mate, devices)
    d_queries = (dq_mine + dq_other.astype(F32)).astype(BF16)

    arrived = home_a.astype(F32) + home_b.astype(F32) + own_a + own_b
    mine_in = jnp.where(odd, arrived[:, rows:], arrived[:, :rows])
    mate_in = jnp.where(odd, arrived[:, :rows], arrived[:, rows:])
    from_mate = swap(mate_in.astype(BF16), devices)
    total = (mine_in + from_mate.astype(F32)).astype(BF16)
    return d_queries, total[0], total[1]


def solution(mesh):
    spec = P(AXES, None)
    return jax.shard_map(
        local_grads,
        mesh=mesh,
        in_specs=(spec, spec, spec, spec, P()),
        out_specs=(spec, spec, spec),
        check_vma=False,
    )
```

```python
import functools
import itertools
import math

import jax
import jax.numpy as jnp
from jax import lax
from jax.experimental import pallas as pl
from jax.experimental.pallas import tpu as pltpu
from jax.sharding import PartitionSpec as P

HEAD_SIZE = 128
GROUP = 8
AXES = ("dp", "seq")
NEG = -1e30
FAR = 1 << 30
NEAR_STEPS = (1, 2)
FAR_STEP = 3
SCALE = 1.0 / math.sqrt(HEAD_SIZE)
SCALE2 = SCALE * math.log2(math.e)
F32 = jnp.float32
BF16 = jnp.bfloat16


def ring(devices, steps):
    moves = [(d, d + 2 * steps[d % 2]) for d in range(devices)]
    inside = [(s, t) for s, t in moves if t < devices]
    sources = [s for s, t in moves if t >= devices]
    targets = sorted(set(range(devices)) - {t for _, t in inside})

    def turns(s, t):
        return bin((s // 2 ^ t // 2) & 3).count("1")

    def cost(order):
        found = [turns(s, t) for s, t in zip(sources, order)]
        return max(found), sum(found)

    return inside + list(zip(sources, min(itertools.permutations(targets), key=cost)))


def swap(value, devices):
    return lax.ppermute(value, AXES, [(d, d ^ 1) for d in range(devices)])


def dot_nt(a, b):
    return lax.dot_general(a, b, (((1,), (1,)), ((), ())), preferred_element_type=F32)


def dot_nn(a, b):
    return lax.dot_general(a, b, (((1,), (0,)), ((), ())), preferred_element_type=F32)


def where_am_i():
    me = lax.axis_index("dp") * lax.axis_size("seq") + lax.axis_index("seq")
    return me, lax.rem(me, 2) == 1


def prepare_kernel(
    rows, lens_hbm, q_hbm, g_hbm, q_ref, g_ref, member_ref, late_ref, lens_ref, lens_sem, q_sem, g_sem
):
    t = rows
    fetch = pltpu.make_async_copy(lens_hbm, lens_ref, lens_sem)
    fetch.start()
    stacks = []
    for h in range(q_hbm.shape[1] // HEAD_SIZE):
        span, lanes = slice(h * t, (h + 1) * t), slice(h * HEAD_SIZE, (h + 1) * HEAD_SIZE)
        for source, target, sem in ((q_hbm, q_ref, q_sem), (g_hbm, g_ref, g_sem)):
            stacks.append(pltpu.make_async_copy(source.at[:, lanes], target.at[span, :], sem.at[h]))
    for stack in stacks:
        stack.start()
    me, odd = where_am_i()
    lane = lax.broadcasted_iota(jnp.int32, (1, HEAD_SIZE), 1)
    down = lax.broadcasted_iota(jnp.int32, (t, HEAD_SIZE), 0)
    near = (me // 2 - jnp.where(odd, 2, 1)) * 2 * t
    starts_of_parts = (((me - 2 * FAR_STEP) * t, me * t), (near, near + t))
    far = jnp.full((1, HEAD_SIZE), FAR, jnp.int32)
    zero = jnp.int32(0)
    fetch.wait()
    for side in (0, 1):
        first = (me if side == 0 else jnp.where(odd, me - 1, me + 1)) * t

        def next_doc(j, carry, first=first):
            end, count, starts, stops = carry
            begin, end = end, end + lens_ref[j]
            live = end > first
            here = (lane == count) & live
            starts, stops = jnp.where(here, begin, starts), jnp.where(here, end, stops)
            return end, count + live.astype(jnp.int32), starts, stops

        _, _, starts, stops = lax.fori_loop(0, lens_ref.shape[0], next_doc, (zero, zero, far, far))
        q_pos = first + down
        member = jnp.where((q_pos >= starts) & (q_pos < stops), 1.0, 0.0).astype(BF16)
        member_ref[side, :t, :] = member
        member_ref[side, t:, :] = member
        for block in (0, 1):
            for part in (0, 1):
                k_pos = starts_of_parts[block][part] + down
                blocked = (k_pos < starts) | (k_pos >= first + t)
                late_ref[block, side, part * t : (part + 1) * t, :] = jnp.where(
                    blocked, NEG, 0.0
                ).astype(BF16)
    for stack in stacks:
        stack.wait()


def stacked(ref, rows, first_head, count):
    return ref[first_head * rows : (first_head + count) * rows, :]


def block_rows(block, kind, mine_ref, got_ref, lanes):
    if block:
        return got_ref[kind, :, lanes]
    return jnp.concatenate([got_ref[kind, :, lanes], mine_ref[kind, :, lanes]], axis=0)


def combine(one, two):
    high = jnp.maximum(one[0], two[0])
    keep_one, keep_two = jnp.exp2(one[0] - high), jnp.exp2(two[0] - high)
    return high, one[1] * keep_one + two[1] * keep_two, one[2] * keep_one + two[2] * keep_two


def score_kernel(rows, block, *refs):
    qs, gs = (refs[0], refs[2]), (refs[1], refs[3])
    member_ref, late_ref, mine_ref, got_ref = refs[4:8]
    before_ref = refs[8] if block else None
    s_ref, g_ref, stats_ref = refs[-3:]
    t = rows
    causal = lax.broadcasted_iota(jnp.int32, (t, t), 0) <= lax.broadcasted_iota(
        jnp.int32, (t, t), 1
    )
    causal = jnp.concatenate([causal, causal], axis=1)

    def fold(x, op):
        return op(x.reshape(-1, 8, 2 * t), axis=0)

    for head in range(mine_ref.shape[2] // HEAD_SIZE):
        lanes = slice(head * HEAD_SIZE, (head + 1) * HEAD_SIZE)
        key, value = (block_rows(block, kind, mine_ref, got_ref, lanes) for kind in (0, 1))
        for side in (0, 1):
            key_late = jnp.concatenate([key, late_ref[block, side]], axis=1)
            for pair in range(GROUP // 2):
                cols = slice((side * GROUP + pair * 2) * t, (side * GROUP + pair * 2 + 2) * t)
                q_rows = stacked(qs[side], t, head * GROUP + pair * 2, 2)
                q_rows = jnp.concatenate([q_rows, member_ref[side]], axis=1)
                s = dot_nt(key_late, q_rows) * SCALE2
                g = dot_nt(value, stacked(gs[side], t, head * GROUP + pair * 2, 2))
                parts = [s[:t], s[t:]]
                if block == 0 and side == 0:
                    parts[1] = jnp.where(causal, parts[1], NEG)
                s_ref[head, :t, cols] = parts[0]
                s_ref[head, t:, cols] = parts[1]
                g_ref[head, :, cols] = g
                top = jnp.maximum(fold(parts[0], jnp.max), fold(parts[1], jnp.max))
                top = jnp.max(top, axis=0, keepdims=True)
                total = jnp.zeros((8, 2 * t), F32)
                weighted = jnp.zeros((8, 2 * t), F32)
                for part in (0, 1):
                    e = jnp.exp2(parts[part] - top)
                    total += fold(e, jnp.sum)
                    weighted += fold(e * g[part * t : (part + 1) * t], jnp.sum)
                turn = side * (GROUP // 2) + pair
                for i, found in enumerate((total, weighted)):
                    stats_ref[3 * head + 1 + i, turn : turn + 1, :] = jnp.sum(
                        found, axis=0, keepdims=True
                    )
                stats_ref[3 * head, turn : turn + 1, :] = top
        if block:
            found = combine(*([ref[3 * head + i] for i in range(3)] for ref in (stats_ref, before_ref)))
            for i in range(3):
                stats_ref[3 * head + i] = found[i]


def grads_kernel(rows, block, *refs):
    qs, gs = (refs[0], refs[2]), (refs[1], refs[3])
    s_ref, g_ref, stats_ref, other_ref, ds_ref, home_ref = refs[4:10]
    t = rows
    for head in range(s_ref.shape[0]):
        lanes = slice(head * HEAD_SIZE, (head + 1) * HEAD_SIZE)
        mine = [stats_ref[3 * head + i] for i in range(3)]
        half = GROUP // 2
        mates = [other_ref[3 * head + i] for i in range(3)]
        mates = [jnp.concatenate([x[half:], x[:half]], axis=0) for x in mates]
        high, total, weighted = combine(mine, mates)
        levels, deltas = high + jnp.log2(total), weighted / total
        grads = [None, None]
        for side in (0, 1):
            for pair in range(half):
                turn = side * half + pair
                cols = slice(turn * 2 * t, (turn + 1) * 2 * t)
                level, delta = levels[turn : turn + 1], deltas[turn : turn + 1]
                p = jnp.exp2(s_ref[head, :, cols] - level)
                ds = (p * (g_ref[head, :, cols] - delta)).astype(BF16)
                ds_ref[head, :, cols] = ds
                at = head * GROUP + pair * 2
                dk = dot_nn(ds, stacked(qs[side], t, at, 2))
                dv = dot_nn(p.astype(BF16), stacked(gs[side], t, at, 2))
                grads = [dk, dv] if turn == 0 else [grads[0] + dk, grads[1] + dv]
        grads[0] = grads[0] * SCALE
        for kind, grad in enumerate(grads):
            if block:
                home_ref[kind, :, lanes] = grad.astype(BF16)
            else:
                home_ref[kind, :, lanes] = grad[:t].astype(BF16)
                refs[10][kind, :, lanes] = grad[t:]


def query_kernel(rows, kv_ref, b_ref, a_ref, dsb_ref, dsa_ref, mine_ref, mate_ref):
    t = rows
    for head in range(dsb_ref.shape[0]):
        lanes = slice(head * HEAD_SIZE, (head + 1) * HEAD_SIZE)
        key_b, key_a = (
            block_rows(block, 0, kv_ref, got, lanes).T for block, got in ((0, b_ref), (1, a_ref))
        )
        for side, out_ref in ((1, mate_ref), (0, mine_ref)):
            cols = slice(side * GROUP * t, (side + 1) * GROUP * t)
            dqt = dot_nn(key_b, dsb_ref[head, :, cols]) + dot_nn(key_a, dsa_ref[head, :, cols])
            dqt = dqt * SCALE
            for h in range(GROUP):
                at = (head * GROUP + h) * HEAD_SIZE
                out_ref[:, at : at + HEAD_SIZE] = dqt[:, h * t : (h + 1) * t].T.astype(out_ref.dtype)


def local_grads(queries, keys, values, d_out, doc_lengths):
    rows, q_width = queries.shape
    kv_width = keys.shape[1]
    kv_heads = kv_width // HEAD_SIZE
    devices = lax.axis_size("dp") * lax.axis_size("seq")
    _, odd = where_am_i()
    a_moves, b_moves = ring(devices, NEAR_STEPS), ring(devices, (FAR_STEP, FAR_STEP))

    mine = lax.optimization_barrier(jnp.stack([keys, values]))
    mate = swap(mine, devices)
    b = lax.ppermute(mine, AXES, b_moves)
    full = jnp.concatenate([jnp.where(odd, mate, mine), jnp.where(odd, mine, mate)], axis=1)
    a = lax.ppermute(full, AXES, a_moves)

    shape = jax.ShapeDtypeStruct
    in_vmem = pl.BlockSpec(memory_space=pltpu.VMEM)
    grant = pltpu.CompilerParams(vmem_limit_bytes=(12 + 10 * kv_heads) << 20)

    def cost(flops):
        return pl.CostEstimate(flops=flops, bytes_accessed=1 << 20, transcendentals=0)

    width = 2 * GROUP * rows
    mine_q, mine_g, member, late = pl.pallas_call(
        functools.partial(prepare_kernel, rows),
        in_specs=[pl.BlockSpec(memory_space=pltpu.HBM)] * 3,
        out_specs=[in_vmem] * 4,
        out_shape=[
            shape((q_width // HEAD_SIZE * rows, HEAD_SIZE), BF16),
            shape((q_width // HEAD_SIZE * rows, HEAD_SIZE), BF16),
            shape((2, 2 * rows, HEAD_SIZE), BF16),
            shape((2, 2, 2 * rows, HEAD_SIZE), BF16),
        ],
        scratch_shapes=[
            pltpu.SMEM(doc_lengths.shape, jnp.int32),
            pltpu.SemaphoreType.DMA,
            *[pltpu.SemaphoreType.DMA((q_width // HEAD_SIZE,))] * 2,
        ],
        compiler_params=grant,
        cost_estimate=cost(1 << 20),
    )(*(pltpu.with_memory_space_constraint(x, pltpu.HBM) for x in (doc_lengths, queries, d_out)))

    mate_q = swap(mine_q, devices)
    mate_g = swap(mine_g, devices)

    rows_of = (mine_q, mine_g, mate_q, mate_g)

    def scores(block, got, *before):
        return pl.pallas_call(
            functools.partial(score_kernel, rows, block),
            in_specs=[in_vmem] * (8 + len(before)),
            out_specs=[in_vmem] * 3,
            out_shape=[
                shape((kv_heads, 2 * rows, width), F32),
                shape((kv_heads, 2 * rows, width), F32),
                shape((3 * kv_heads, GROUP, 2 * rows), F32),
            ],
            compiler_params=grant,
            cost_estimate=cost(1 << 28),
        )(*rows_of, member, late, mine, got, *before)

    def grads(block, s, g, stats, other):
        out_shape = [shape((kv_heads, 2 * rows, width), BF16)]
        if block:
            out_shape += [shape((2, 2 * rows, kv_width), BF16)]
        else:
            out_shape += [shape((2, rows, kv_width), BF16), shape((2, rows, kv_width), F32)]
        return pl.pallas_call(
            functools.partial(grads_kernel, rows, block),
            in_specs=[in_vmem] * 8,
            out_specs=[in_vmem] * len(out_shape),
            out_shape=out_shape,
            compiler_params=grant,
            cost_estimate=cost(1 << 28),
        )(*rows_of, s, g, stats, other)

    s_b, g_b, stats_b = scores(0, b)
    s_a, g_a, stats = scores(1, a, stats_b)
    other = swap(stats, devices)
    ds_a, back_a = grads(1, s_a, g_a, stats, other)
    home_a = lax.ppermute(back_a, AXES, [(d, s) for s, d in a_moves])
    ds_b, back_b, own = grads(0, s_b, g_b, stats, other)
    home_b = lax.ppermute(back_b, AXES, [(d, s) for s, d in b_moves])
    dq_mine, dq_mate = pl.pallas_call(
        functools.partial(query_kernel, rows),
        in_specs=[in_vmem] * 5,
        out_specs=[in_vmem] * 2,
        out_shape=[shape((rows, q_width), F32), shape((rows, q_width), BF16)],
        compiler_params=grant,
        cost_estimate=cost(1 << 28),
    )(mine, b, a, ds_b, ds_a)
    dq_other = swap(dq_mate, devices)
    d_queries = (dq_mine + dq_other.astype(F32)).astype(BF16)

    first, second = home_a[:, :rows].astype(F32), home_a[:, rows:].astype(F32)
    from_mate = swap(jnp.where(odd, first, second).astype(BF16), devices)
    total = own + home_b.astype(F32) + jnp.where(odd, second, first) + from_mate.astype(F32)
    total = total.astype(BF16)
    return d_queries, total[0], total[1]


def solution(mesh):
    spec = P(AXES, None)
    return jax.shard_map(
        local_grads,
        mesh=mesh,
        in_specs=(spec, spec, spec, spec, P()),
        out_specs=(spec, spec, spec),
        check_vma=False,
    )
```

```python
import functools
import itertools
import math

import jax
import jax.numpy as jnp
from jax import lax
from jax.experimental import pallas as pl
from jax.experimental.pallas import tpu as pltpu
from jax.sharding import PartitionSpec as P

HEAD_SIZE = 128
GROUP = 8
AXES = ("dp", "seq")
NEG = -1e30
FAR = 1 << 30
NEAR_STEPS = (1, 3)
FAR_STEP = 2
SCALE = 1.0 / math.sqrt(HEAD_SIZE)
SCALE2 = SCALE * math.log2(math.e)
F32 = jnp.float32
BF16 = jnp.bfloat16


def ring(devices, steps):
    moves = [(d, d + 2 * steps[d % 2]) for d in range(devices)]
    inside = [(s, t) for s, t in moves if t < devices]
    sources = [s for s, t in moves if t >= devices]
    targets = sorted(set(range(devices)) - {t for _, t in inside})

    def turns(s, t):
        return bin((s // 2 ^ t // 2) & 3).count("1")

    def cost(order):
        found = [turns(s, t) for s, t in zip(sources, order)]
        return max(found), sum(found)

    return inside + list(zip(sources, min(itertools.permutations(targets), key=cost)))


def swap(value, devices):
    return lax.ppermute(value, AXES, [(d, d ^ 1) for d in range(devices)])


def dot_nt(a, b):
    return lax.dot_general(a, b, (((1,), (1,)), ((), ())), preferred_element_type=F32)


def dot_nn(a, b):
    return lax.dot_general(a, b, (((1,), (0,)), ((), ())), preferred_element_type=F32)


def where_am_i():
    me = lax.axis_index("dp") * lax.axis_size("seq") + lax.axis_index("seq")
    return me, lax.rem(me, 2) == 1


def prepare_kernel(
    rows, lens_hbm, q_hbm, g_hbm, q_ref, g_ref, member_ref, late_ref, lens_ref, lens_sem, q_sem, g_sem
):
    t = rows
    fetch = pltpu.make_async_copy(lens_hbm, lens_ref, lens_sem)
    fetch.start()
    stacks = []
    for h in range(q_hbm.shape[1] // HEAD_SIZE):
        span, lanes = slice(h * t, (h + 1) * t), slice(h * HEAD_SIZE, (h + 1) * HEAD_SIZE)
        for source, target, sem in ((q_hbm, q_ref, q_sem), (g_hbm, g_ref, g_sem)):
            stacks.append(pltpu.make_async_copy(source.at[:, lanes], target.at[span, :], sem.at[h]))
    for stack in stacks:
        stack.start()
    me, odd = where_am_i()
    lane = lax.broadcasted_iota(jnp.int32, (1, HEAD_SIZE), 1)
    down = lax.broadcasted_iota(jnp.int32, (t, HEAD_SIZE), 0)
    near = (me // 2 - jnp.where(odd, NEAR_STEPS[1], NEAR_STEPS[0])) * 2 * t
    starts_of_parts = (((me - 2 * FAR_STEP) * t, me * t), (near, near + t))
    far = jnp.full((1, HEAD_SIZE), FAR, jnp.int32)
    zero = jnp.int32(0)
    fetch.wait()
    for side in (0, 1):
        first = (me if side == 0 else jnp.where(odd, me - 1, me + 1)) * t

        def next_doc(j, carry, first=first):
            end, count, starts, stops = carry
            begin, end = end, end + lens_ref[j]
            live = end > first
            here = (lane == count) & live
            starts, stops = jnp.where(here, begin, starts), jnp.where(here, end, stops)
            return end, count + live.astype(jnp.int32), starts, stops

        _, _, starts, stops = lax.fori_loop(0, lens_ref.shape[0], next_doc, (zero, zero, far, far))
        q_pos = first + down
        member = jnp.where((q_pos >= starts) & (q_pos < stops), 1.0, 0.0).astype(BF16)
        member_ref[side, :t, :] = member
        member_ref[side, t:, :] = member
        for block in (0, 1):
            for part in (0, 1):
                k_pos = starts_of_parts[block][part] + down
                blocked = (k_pos < starts) | (k_pos >= first + t)
                late_ref[block, side, part * t : (part + 1) * t, :] = jnp.where(
                    blocked, NEG, 0.0
                ).astype(BF16)
    for stack in stacks:
        stack.wait()


def stacked(ref, rows, first_head, count):
    return ref[first_head * rows : (first_head + count) * rows, :]


def block_rows(block, kind, mine_ref, got_ref, lanes):
    if block:
        return got_ref[kind, :, lanes]
    return jnp.concatenate([got_ref[kind, :, lanes], mine_ref[kind, :, lanes]], axis=0)


def combine(one, two):
    high = jnp.maximum(one[0], two[0])
    keep_one, keep_two = jnp.exp2(one[0] - high), jnp.exp2(two[0] - high)
    return high, one[1] * keep_one + two[1] * keep_two, one[2] * keep_one + two[2] * keep_two


def score_kernel(rows, block, *refs):
    qs, gs = (refs[0], refs[2]), (refs[1], refs[3])
    member_ref, late_ref, mine_ref, got_ref = refs[4:8]
    before_ref = refs[8] if block else None
    s_ref, g_ref, stats_ref = refs[-3:]
    t = rows
    causal = lax.broadcasted_iota(jnp.int32, (t, t), 0) <= lax.broadcasted_iota(
        jnp.int32, (t, t), 1
    )
    causal = jnp.concatenate([causal, causal], axis=1)

    def fold(x, op):
        return op(x.reshape(-1, 8, 2 * t), axis=0)

    for head in range(mine_ref.shape[2] // HEAD_SIZE):
        lanes = slice(head * HEAD_SIZE, (head + 1) * HEAD_SIZE)
        key, value = (block_rows(block, kind, mine_ref, got_ref, lanes) for kind in (0, 1))
        for side in (0, 1):
            key_late = jnp.concatenate([key, late_ref[block, side]], axis=1)
            for pair in range(GROUP // 2):
                cols = slice((side * GROUP + pair * 2) * t, (side * GROUP + pair * 2 + 2) * t)
                q_rows = stacked(qs[side], t, head * GROUP + pair * 2, 2)
                q_rows = jnp.concatenate([q_rows, member_ref[side]], axis=1)
                s = dot_nt(key_late, q_rows) * SCALE2
                g = dot_nt(value, stacked(gs[side], t, head * GROUP + pair * 2, 2))
                parts = [s[:t], s[t:]]
                if block == 0 and side == 0:
                    parts[1] = jnp.where(causal, parts[1], NEG)
                s_ref[head, :t, cols] = parts[0]
                s_ref[head, t:, cols] = parts[1]
                g_ref[head, :, cols] = g
                top = jnp.maximum(fold(parts[0], jnp.max), fold(parts[1], jnp.max))
                top = jnp.max(top, axis=0, keepdims=True)
                total = jnp.zeros((8, 2 * t), F32)
                weighted = jnp.zeros((8, 2 * t), F32)
                for part in (0, 1):
                    e = jnp.exp2(parts[part] - top)
                    total += fold(e, jnp.sum)
                    weighted += fold(e * g[part * t : (part + 1) * t], jnp.sum)
                turn = side * (GROUP // 2) + pair
                for i, found in enumerate((total, weighted)):
                    stats_ref[3 * head + 1 + i, turn : turn + 1, :] = jnp.sum(
                        found, axis=0, keepdims=True
                    )
                stats_ref[3 * head, turn : turn + 1, :] = top
        if block:
            found = combine(*([ref[3 * head + i] for i in range(3)] for ref in (stats_ref, before_ref)))
            for i in range(3):
                stats_ref[3 * head + i] = found[i]


def grads_kernel(rows, block, *refs):
    qs, gs = (refs[0], refs[2]), (refs[1], refs[3])
    s_ref, g_ref, stats_ref, other_ref, ds_ref, home_ref = refs[4:10]
    t = rows
    for head in range(s_ref.shape[0]):
        lanes = slice(head * HEAD_SIZE, (head + 1) * HEAD_SIZE)
        mine = [stats_ref[3 * head + i] for i in range(3)]
        half = GROUP // 2
        mates = [other_ref[3 * head + i] for i in range(3)]
        mates = [jnp.concatenate([x[half:], x[:half]], axis=0) for x in mates]
        high, total, weighted = combine(mine, mates)
        levels, deltas = high + jnp.log2(total), weighted / total
        grads = [None, None]
        for side in (0, 1):
            for pair in range(half):
                turn = side * half + pair
                cols = slice(turn * 2 * t, (turn + 1) * 2 * t)
                level, delta = levels[turn : turn + 1], deltas[turn : turn + 1]
                p = jnp.exp2(s_ref[head, :, cols] - level)
                ds = (p * (g_ref[head, :, cols] - delta)).astype(BF16)
                ds_ref[head, :, cols] = ds
                at = head * GROUP + pair * 2
                dk = dot_nn(ds, stacked(qs[side], t, at, 2))
                dv = dot_nn(p.astype(BF16), stacked(gs[side], t, at, 2))
                grads = [dk, dv] if turn == 0 else [grads[0] + dk, grads[1] + dv]
        grads[0] = grads[0] * SCALE
        for kind, grad in enumerate(grads):
            if block:
                home_ref[kind, :, lanes] = grad.astype(BF16)
            else:
                home_ref[kind, :, lanes] = grad[:t].astype(BF16)
                refs[10][kind, :, lanes] = grad[t:]


def query_kernel(rows, kv_ref, b_ref, a_ref, dsb_ref, dsa_ref, mine_ref, mate_ref):
    t = rows
    for head in range(dsb_ref.shape[0]):
        lanes = slice(head * HEAD_SIZE, (head + 1) * HEAD_SIZE)
        key_b, key_a = (
            block_rows(block, 0, kv_ref, got, lanes).T for block, got in ((0, b_ref), (1, a_ref))
        )
        for side, out_ref in ((1, mate_ref), (0, mine_ref)):
            cols = slice(side * GROUP * t, (side + 1) * GROUP * t)
            dqt = dot_nn(key_b, dsb_ref[head, :, cols]) + dot_nn(key_a, dsa_ref[head, :, cols])
            dqt = dqt * SCALE
            for h in range(GROUP):
                at = (head * GROUP + h) * HEAD_SIZE
                out_ref[:, at : at + HEAD_SIZE] = dqt[:, h * t : (h + 1) * t].T.astype(out_ref.dtype)


def local_grads(queries, keys, values, d_out, doc_lengths):
    rows, q_width = queries.shape
    kv_width = keys.shape[1]
    kv_heads = kv_width // HEAD_SIZE
    devices = lax.axis_size("dp") * lax.axis_size("seq")
    _, odd = where_am_i()
    a_moves, b_moves = ring(devices, NEAR_STEPS), ring(devices, (FAR_STEP, FAR_STEP))

    mine = lax.optimization_barrier(jnp.stack([keys, values]))
    mate = swap(mine, devices)
    b = lax.ppermute(mine, AXES, b_moves)
    full = jnp.concatenate([jnp.where(odd, mate, mine), jnp.where(odd, mine, mate)], axis=1)
    a = lax.ppermute(full, AXES, a_moves)

    shape = jax.ShapeDtypeStruct
    in_vmem = pl.BlockSpec(memory_space=pltpu.VMEM)
    grant = pltpu.CompilerParams(vmem_limit_bytes=(12 + 10 * kv_heads) << 20)

    def cost(flops):
        return pl.CostEstimate(flops=flops, bytes_accessed=1 << 20, transcendentals=0)

    width = 2 * GROUP * rows
    mine_q, mine_g, member, late = pl.pallas_call(
        functools.partial(prepare_kernel, rows),
        in_specs=[pl.BlockSpec(memory_space=pltpu.HBM)] * 3,
        out_specs=[in_vmem] * 4,
        out_shape=[
            shape((q_width // HEAD_SIZE * rows, HEAD_SIZE), BF16),
            shape((q_width // HEAD_SIZE * rows, HEAD_SIZE), BF16),
            shape((2, 2 * rows, HEAD_SIZE), BF16),
            shape((2, 2, 2 * rows, HEAD_SIZE), BF16),
        ],
        scratch_shapes=[
            pltpu.SMEM(doc_lengths.shape, jnp.int32),
            pltpu.SemaphoreType.DMA,
            *[pltpu.SemaphoreType.DMA((q_width // HEAD_SIZE,))] * 2,
        ],
        compiler_params=grant,
        cost_estimate=cost(1 << 20),
    )(*(pltpu.with_memory_space_constraint(x, pltpu.HBM) for x in (doc_lengths, queries, d_out)))

    mate_q = swap(mine_q, devices)
    mate_g = swap(mine_g, devices)

    rows_of = (mine_q, mine_g, mate_q, mate_g)

    def scores(block, got, *before):
        return pl.pallas_call(
            functools.partial(score_kernel, rows, block),
            in_specs=[in_vmem] * (8 + len(before)),
            out_specs=[in_vmem] * 3,
            out_shape=[
                shape((kv_heads, 2 * rows, width), F32),
                shape((kv_heads, 2 * rows, width), F32),
                shape((3 * kv_heads, GROUP, 2 * rows), F32),
            ],
            compiler_params=grant,
            cost_estimate=cost(1 << 28),
        )(*rows_of, member, late, mine, got, *before)

    def grads(block, s, g, stats, other):
        out_shape = [shape((kv_heads, 2 * rows, width), BF16)]
        if block:
            out_shape += [shape((2, 2 * rows, kv_width), BF16)]
        else:
            out_shape += [shape((2, rows, kv_width), BF16), shape((2, rows, kv_width), F32)]
        return pl.pallas_call(
            functools.partial(grads_kernel, rows, block),
            in_specs=[in_vmem] * 8,
            out_specs=[in_vmem] * len(out_shape),
            out_shape=out_shape,
            compiler_params=grant,
            cost_estimate=cost(1 << 28),
        )(*rows_of, s, g, stats, other)

    s_b, g_b, stats_b = scores(0, b)
    s_a, g_a, stats = scores(1, a, stats_b)
    other = swap(stats, devices)
    ds_a, back_a = grads(1, s_a, g_a, stats, other)
    home_a = lax.ppermute(back_a, AXES, [(d, s) for s, d in a_moves])
    ds_b, back_b, own = grads(0, s_b, g_b, stats, other)
    home_b = lax.ppermute(back_b, AXES, [(d, s) for s, d in b_moves])
    dq_mine, dq_mate = pl.pallas_call(
        functools.partial(query_kernel, rows),
        in_specs=[in_vmem] * 5,
        out_specs=[in_vmem] * 2,
        out_shape=[shape((rows, q_width), F32), shape((rows, q_width), BF16)],
        compiler_params=grant,
        cost_estimate=cost(1 << 28),
    )(mine, b, a, ds_b, ds_a)
    dq_other = swap(dq_mate, devices)
    d_queries = (dq_mine + dq_other.astype(F32)).astype(BF16)

    first, second = home_a[:, :rows].astype(F32), home_a[:, rows:].astype(F32)
    from_mate = swap(jnp.where(odd, first, second).astype(BF16), devices)
    total = own + home_b.astype(F32) + jnp.where(odd, second, first) + from_mate.astype(F32)
    total = total.astype(BF16)
    return d_queries, total[0], total[1]


def solution(mesh):
    spec = P(AXES, None)
    return jax.shard_map(
        local_grads,
        mesh=mesh,
        in_specs=(spec, spec, spec, spec, P()),
        out_specs=(spec, spec, spec),
        check_vma=False,
    )
```

```python
import functools
import itertools
import math

import jax
import jax.numpy as jnp
from jax import lax
from jax.experimental import pallas as pl
from jax.experimental.pallas import tpu as pltpu
from jax.sharding import PartitionSpec as P

HEAD_SIZE = 128
GROUP = 8
AXES = ("dp", "seq")
NEG = -1e30
FAR = 1 << 30
NEAR_STEPS = (1, 3)
FAR_STEP = 2
SCALE = 1.0 / math.sqrt(HEAD_SIZE)
SCALE2 = SCALE * math.log2(math.e)
F32 = jnp.float32
BF16 = jnp.bfloat16


def ring(devices, steps):
    moves = [(d, d + 2 * steps[d % 2]) for d in range(devices)]
    inside = [(s, t) for s, t in moves if t < devices]
    sources = [s for s, t in moves if t >= devices]
    targets = sorted(set(range(devices)) - {t for _, t in inside})

    def turns(s, t):
        return bin((s // 2 ^ t // 2) & 3).count("1")

    def cost(order):
        found = [turns(s, t) for s, t in zip(sources, order)]
        return max(found), sum(found)

    return inside + list(zip(sources, min(itertools.permutations(targets), key=cost)))


def swap(value, devices):
    return lax.ppermute(value, AXES, [(d, d ^ 1) for d in range(devices)])


def dot_nt(a, b):
    return lax.dot_general(a, b, (((1,), (1,)), ((), ())), preferred_element_type=F32)


def dot_nn(a, b):
    return lax.dot_general(a, b, (((1,), (0,)), ((), ())), preferred_element_type=F32)


def where_am_i():
    me = lax.axis_index("dp") * lax.axis_size("seq") + lax.axis_index("seq")
    return me, lax.rem(me, 2) == 1


def prepare_kernel(
    rows, lens_hbm, q_hbm, g_hbm, q_ref, g_ref, member_ref, late_ref, lens_ref, lens_sem, q_sem, g_sem
):
    t = rows
    fetch = pltpu.make_async_copy(lens_hbm, lens_ref, lens_sem)
    fetch.start()
    stacks = []
    for h in range(q_hbm.shape[1] // HEAD_SIZE):
        span, lanes = slice(h * t, (h + 1) * t), slice(h * HEAD_SIZE, (h + 1) * HEAD_SIZE)
        for source, target, sem in ((q_hbm, q_ref, q_sem), (g_hbm, g_ref, g_sem)):
            stacks.append(pltpu.make_async_copy(source.at[:, lanes], target.at[span, :], sem.at[h]))
    for stack in stacks:
        stack.start()
    me, odd = where_am_i()
    lane = lax.broadcasted_iota(jnp.int32, (1, HEAD_SIZE), 1)
    down = lax.broadcasted_iota(jnp.int32, (t, HEAD_SIZE), 0)
    near = (me // 2 - jnp.where(odd, NEAR_STEPS[1], NEAR_STEPS[0])) * 2 * t
    starts_of_parts = (((me - 2 * FAR_STEP) * t, me * t), (near, near + t))
    far = jnp.full((1, HEAD_SIZE), FAR, jnp.int32)
    zero = jnp.int32(0)
    fetch.wait()
    for side in (0, 1):
        first = (me if side == 0 else jnp.where(odd, me - 1, me + 1)) * t

        def next_doc(j, carry, first=first):
            end, count, starts, stops = carry
            begin, end = end, end + lens_ref[j]
            live = end > first
            here = (lane == count) & live
            starts, stops = jnp.where(here, begin, starts), jnp.where(here, end, stops)
            return end, count + live.astype(jnp.int32), starts, stops

        _, _, starts, stops = lax.fori_loop(0, lens_ref.shape[0], next_doc, (zero, zero, far, far))
        q_pos = first + down
        member = jnp.where((q_pos >= starts) & (q_pos < stops), 1.0, 0.0).astype(BF16)
        member_ref[side, :t, :] = member
        member_ref[side, t:, :] = member
        for block in (0, 1):
            for part in (0, 1):
                k_pos = starts_of_parts[block][part] + down
                blocked = (k_pos < starts) | (k_pos >= first + t)
                late_ref[block, side, part * t : (part + 1) * t, :] = jnp.where(
                    blocked, NEG, 0.0
                ).astype(BF16)
    for stack in stacks:
        stack.wait()


def stacked(ref, rows, first_head, count):
    return ref[first_head * rows : (first_head + count) * rows, :]


def block_rows(block, kind, mine_ref, got_ref, lanes):
    if block:
        return got_ref[kind, :, lanes]
    return jnp.concatenate([got_ref[kind, :, lanes], mine_ref[kind, :, lanes]], axis=0)


def combine(one, two):
    high = jnp.maximum(one[0], two[0])
    keep_one, keep_two = jnp.exp2(one[0] - high), jnp.exp2(two[0] - high)
    return high, one[1] * keep_one + two[1] * keep_two, one[2] * keep_one + two[2] * keep_two


def score_kernel(rows, block, *refs):
    qs, gs = (refs[0], refs[2]), (refs[1], refs[3])
    member_ref, late_ref, mine_ref, got_ref = refs[4:8]
    before_ref = refs[8] if block else None
    s_ref, g_ref, stats_ref = refs[-3:]
    t = rows
    causal = lax.broadcasted_iota(jnp.int32, (t, t), 0) <= lax.broadcasted_iota(
        jnp.int32, (t, t), 1
    )
    causal = jnp.concatenate([causal, causal], axis=1)

    def fold(x, op):
        return op(x.reshape(-1, 8, 2 * t), axis=0)

    for head in range(mine_ref.shape[2] // HEAD_SIZE):
        lanes = slice(head * HEAD_SIZE, (head + 1) * HEAD_SIZE)
        key, value = (block_rows(block, kind, mine_ref, got_ref, lanes) for kind in (0, 1))
        for side in (0, 1):
            key_late = jnp.concatenate([key, late_ref[block, side]], axis=1)
            for pair in range(GROUP // 2):
                cols = slice((side * GROUP + pair * 2) * t, (side * GROUP + pair * 2 + 2) * t)
                q_rows = stacked(qs[side], t, head * GROUP + pair * 2, 2)
                q_rows = jnp.concatenate([q_rows, member_ref[side]], axis=1)
                s = dot_nt(key_late, q_rows) * SCALE2
                g = dot_nt(value, stacked(gs[side], t, head * GROUP + pair * 2, 2))
                parts = [s[:t], s[t:]]
                if block == 0 and side == 0:
                    parts[1] = jnp.where(causal, parts[1], NEG)
                s_ref[head, :t, cols] = parts[0]
                s_ref[head, t:, cols] = parts[1]
                g_ref[head, :, cols] = g
                top = jnp.maximum(fold(parts[0], jnp.max), fold(parts[1], jnp.max))
                top = jnp.max(top, axis=0, keepdims=True)
                total = jnp.zeros((8, 2 * t), F32)
                weighted = jnp.zeros((8, 2 * t), F32)
                for part in (0, 1):
                    e = jnp.exp2(parts[part] - top)
                    total += fold(e, jnp.sum)
                    weighted += fold(e * g[part * t : (part + 1) * t], jnp.sum)
                turn = side * (GROUP // 2) + pair
                for i, found in enumerate((total, weighted)):
                    stats_ref[3 * head + 1 + i, turn : turn + 1, :] = jnp.sum(
                        found, axis=0, keepdims=True
                    )
                stats_ref[3 * head, turn : turn + 1, :] = top
        if block:
            found = combine(*([ref[3 * head + i] for i in range(3)] for ref in (stats_ref, before_ref)))
            for i in range(3):
                stats_ref[3 * head + i] = found[i]


def grads_kernel(rows, span, *refs):
    qs, gs = (refs[0], refs[2]), (refs[1], refs[3])
    s_ref, g_ref, stats_ref, other_ref, ds_ref, home_ref = refs[4:]
    t = rows
    for head in range(s_ref.shape[0]):
        lanes = slice(head * HEAD_SIZE, (head + 1) * HEAD_SIZE)
        mine = [stats_ref[3 * head + i] for i in range(3)]
        half = GROUP // 2
        mates = [other_ref[3 * head + i] for i in range(3)]
        mates = [jnp.concatenate([x[half:], x[:half]], axis=0) for x in mates]
        high, total, weighted = combine(mine, mates)
        levels, deltas = high + jnp.log2(total), weighted / total
        grads = [None, None]
        for side in (0, 1):
            for pair in range(half):
                turn = side * half + pair
                cols = slice(turn * 2 * t, (turn + 1) * 2 * t)
                level, delta = levels[turn : turn + 1], deltas[turn : turn + 1]
                p = jnp.exp2(s_ref[head, span, cols] - level)
                ds = (p * (g_ref[head, span, cols] - delta)).astype(BF16)
                ds_ref[head, :, cols] = ds
                at = head * GROUP + pair * 2
                dk = dot_nn(ds, stacked(qs[side], t, at, 2))
                dv = dot_nn(p.astype(BF16), stacked(gs[side], t, at, 2))
                grads = [dk, dv] if turn == 0 else [grads[0] + dk, grads[1] + dv]
        grads[0] = grads[0] * SCALE
        for kind, grad in enumerate(grads):
            home_ref[kind, :, lanes] = grad.astype(home_ref.dtype)


def query_kernel(rows, side, *refs):
    t = rows
    keys, scores, out_ref = refs[:3], refs[3:6], refs[6]
    cols = slice(side * GROUP * t, (side + 1) * GROUP * t)
    for head in range(scores[0].shape[0]):
        lanes = slice(head * HEAD_SIZE, (head + 1) * HEAD_SIZE)
        dqt = sum(dot_nn(key[0, :, lanes].T, ds[head, :, cols]) for key, ds in zip(keys, scores))
        dqt = dqt * SCALE
        for h in range(GROUP):
            at = (head * GROUP + h) * HEAD_SIZE
            out_ref[:, at : at + HEAD_SIZE] = dqt[:, h * t : (h + 1) * t].T.astype(out_ref.dtype)


def local_grads(queries, keys, values, d_out, doc_lengths):
    rows, q_width = queries.shape
    kv_width = keys.shape[1]
    kv_heads = kv_width // HEAD_SIZE
    devices = lax.axis_size("dp") * lax.axis_size("seq")
    _, odd = where_am_i()
    a_moves, b_moves = ring(devices, NEAR_STEPS), ring(devices, (FAR_STEP, FAR_STEP))

    mine = lax.optimization_barrier(jnp.stack([keys, values]))
    mate = swap(mine, devices)
    b = lax.ppermute(mine, AXES, b_moves)
    full = jnp.concatenate([jnp.where(odd, mate, mine), jnp.where(odd, mine, mate)], axis=1)
    a = lax.ppermute(full, AXES, a_moves)

    shape = jax.ShapeDtypeStruct
    in_vmem = pl.BlockSpec(memory_space=pltpu.VMEM)
    grant = pltpu.CompilerParams(vmem_limit_bytes=(12 + 10 * kv_heads) << 20)

    def cost(flops):
        return pl.CostEstimate(flops=flops, bytes_accessed=1 << 20, transcendentals=0)

    width = 2 * GROUP * rows
    mine_q, mine_g, member, late = pl.pallas_call(
        functools.partial(prepare_kernel, rows),
        in_specs=[pl.BlockSpec(memory_space=pltpu.HBM)] * 3,
        out_specs=[in_vmem] * 4,
        out_shape=[
            shape((q_width // HEAD_SIZE * rows, HEAD_SIZE), BF16),
            shape((q_width // HEAD_SIZE * rows, HEAD_SIZE), BF16),
            shape((2, 2 * rows, HEAD_SIZE), BF16),
            shape((2, 2, 2 * rows, HEAD_SIZE), BF16),
        ],
        scratch_shapes=[
            pltpu.SMEM(doc_lengths.shape, jnp.int32),
            pltpu.SemaphoreType.DMA,
            *[pltpu.SemaphoreType.DMA((q_width // HEAD_SIZE,))] * 2,
        ],
        compiler_params=grant,
        cost_estimate=cost(1 << 20),
    )(*(pltpu.with_memory_space_constraint(x, pltpu.HBM) for x in (doc_lengths, queries, d_out)))

    mate_q = swap(mine_q, devices)
    mate_g = swap(mine_g, devices)

    rows_of = (mine_q, mine_g, mate_q, mate_g)

    def scores(block, got, *before):
        return pl.pallas_call(
            functools.partial(score_kernel, rows, block),
            in_specs=[in_vmem] * (8 + len(before)),
            out_specs=[in_vmem] * 3,
            out_shape=[
                shape((kv_heads, 2 * rows, width), F32),
                shape((kv_heads, 2 * rows, width), F32),
                shape((3 * kv_heads, GROUP, 2 * rows), F32),
            ],
            compiler_params=grant,
            cost_estimate=cost(1 << 28),
        )(*rows_of, member, late, mine, got, *before)

    s_b, g_b, stats_b = scores(0, b)
    s_a, g_a, stats = scores(1, a, stats_b)
    other = swap(stats, devices)

    def grads(span, dtype, s, g):
        count = span.stop - span.start
        return pl.pallas_call(
            functools.partial(grads_kernel, rows, span),
            in_specs=[in_vmem] * 8,
            out_specs=[in_vmem] * 2,
            out_shape=[
                shape((kv_heads, count, width), BF16),
                shape((2, count, kv_width), dtype),
            ],
            compiler_params=grant,
            cost_estimate=cost(1 << 28),
        )(*rows_of, s, g, stats, other)

    ds_a, back_a = grads(slice(0, 2 * rows), BF16, s_a, g_a)
    home_a = lax.ppermute(back_a, AXES, [(d, s) for s, d in a_moves])
    ds_b, back_b = grads(slice(0, rows), BF16, s_b, g_b)
    home_b = lax.ppermute(back_b, AXES, [(d, s) for s, d in b_moves])
    ds_own, own = grads(slice(rows, 2 * rows), F32, s_b, g_b)

    def query(side, dtype):
        return pl.pallas_call(
            functools.partial(query_kernel, rows, side),
            in_specs=[in_vmem] * 6,
            out_specs=in_vmem,
            out_shape=shape((rows, q_width), dtype),
            compiler_params=grant,
            cost_estimate=cost(1 << 27),
        )(mine, b, a, ds_own, ds_b, ds_a)

    dq_mate = query(1, BF16)
    dq_other = swap(dq_mate, devices)
    dq_mine = query(0, F32)
    d_queries = (dq_mine + dq_other.astype(F32)).astype(BF16)

    first, second = home_a[:, :rows].astype(F32), home_a[:, rows:].astype(F32)
    from_mate = swap(jnp.where(odd, first, second).astype(BF16), devices)
    total = own + home_b.astype(F32) + jnp.where(odd, second, first) + from_mate.astype(F32)
    total = total.astype(BF16)
    return d_queries, total[0], total[1]


def solution(mesh):
    spec = P(AXES, None)
    return jax.shard_map(
        local_grads,
        mesh=mesh,
        in_specs=(spec, spec, spec, spec, P()),
        out_specs=(spec, spec, spec),
        check_vma=False,
    )
```
